32 devices in a mesh: groups: 2 (over x), tm: 16 (over z, y, core).
Axes of the slice: x: 2, y: 2, z: 4, core: 2. Of those that a mesh axis runs over, the one named last changes fastest.
Arguments:
- latent: bfloat16 [64, 8192], P('groups', 'tm'), parts along dimension 0, may hold values from -6 to 6
- w_in: bfloat16 [3, 3, 3, 16, 384], replicated, may hold values from -0.3125 to 0.3125
- b_in: float32 [384], replicated, may hold values from -3 to 3
- gain: float32 [384], replicated, may hold values from 0.1 to 1.9
- w_mid: bfloat16 [3, 3, 3, 384, 384], replicated, may hold values from -0.0625 to 0.0625
- b_mid: float32 [384], replicated, may hold values from -3 to 3
- w_time: bfloat16 [3, 384, 768], replicated, may hold values from -0.1875 to 0.1875
- b_time: float32 [768], replicated, may hold values from -3 to 3
Outputs:
- frames_up: bfloat16 [128, 16, 32, 384], P(('groups', 'tm')), parts along dimension 0
The draws below stay inside these ranges and needn't reach their ends.
There are 2 independent parts, one for each index of `groups`. The reference program is written for one: setup_inputs(seed, part) draws one part's arguments, and reference() takes and returns one part's arrays. A program takes and returns all parts, laid end to end along the dimension named above; an argument that names none is the same for every part. Nothing has to cross between parts.
All inputs are finite; a program needn't handle non-finite values.
Results may differ from the reference program's by a relative error of at most 0.012.
Values may be sent and summed in bfloat16 or wider, within the bound.
A program may use at most 128 MiB of HBM per device.

```python
import jax
import jax.numpy as jnp
from jax import lax

ZC = 16
C = 384
H = 16
W = 32
LF = 32


def shard_levels(key, dims, shards, low, high):
    factor_of, own = 1.0, jax.random.fold_in(key, 6)
    for position, shards_of in shards:
        steps = jnp.exp(jax.random.uniform(jax.random.fold_in(own, position), (shards_of,), jnp.float32, low / len(shards), high / len(shards)))
        factor_of = factor_of * jnp.repeat(steps, dims[position] // shards_of).reshape([-1 if axis == position else 1 for axis in range(len(dims))])
    return factor_of


def noise(rng, dims, scale, bound, split=(), held_as=jnp.bfloat16):
    entries = scale * jax.random.normal(rng, dims, jnp.float32)
    if split:
        entries = entries * shard_levels(rng, dims, split, -0.22, 0.18)
    return jnp.clip(entries, -bound, bound).astype(held_as)


def setup_inputs(seed: int = 0, part: int = 0) -> dict:
    streams_of = jax.random.split(jax.random.key(seed), 9)
    part_splits = jax.random.split(jax.random.fold_in(streams_of[8], part), 9)
    return {
        "latent": noise(part_splits[0], (LF, H * W * ZC), 1.0, 6.0, ((1, 16),)),
        "w_in": noise(streams_of[1], (3, 3, 3, ZC, C), (27 * ZC) ** -0.5, 0.3125),
        "b_in": noise(streams_of[2], (C,), 0.5, 3.0, (), jnp.float32),
        "gain": jnp.clip(1.0 + 0.18 * jax.random.normal(streams_of[3], (C,), jnp.float32), 0.1, 1.9),
        "w_mid": noise(streams_of[4], (3, 3, 3, C, C), (27 * C) ** -0.5, 0.0625),
        "b_mid": noise(streams_of[5], (C,), 0.5, 3.0, (), jnp.float32),
        "w_time": noise(streams_of[6], (3, C, 2 * C), (3 * C) ** -0.5, 0.1875),
        "b_time": noise(streams_of[7], (2 * C,), 0.5, 3.0, (), jnp.float32),
    }


def conv_valid(padded, weight, bias, spatial, edged):
    frames = padded.shape[0] - 2
    rows = padded.shape[1]
    inner = padded.shape[3]
    if spatial:
        margin = 0 if edged else 1
        padded = jnp.pad(padded, ((0, 0), (1, 1), (margin, margin), (0, 0)))
        taps = 3
    else:
        taps = 1
    cols = padded.shape[2] - taps + 1
    total = jnp.zeros((frames * rows * cols, weight.shape[-1]), jnp.float32)
    for step_t in range(3):
        for step_h in range(taps):
            for step_w in range(taps):
                window = padded[step_t:step_t + frames, step_h:step_h + rows, step_w:step_w + cols, :]
                if spatial:
                    kernel = weight[step_t, step_h, step_w]
                else:
                    kernel = weight[step_t]
                total = total + jnp.dot(window.reshape(-1, inner), kernel, preferred_element_type=jnp.float32)
    return (total + bias).reshape(frames, rows, cols, weight.shape[-1])

def conv_input(padded, weight, bias, edged):
    frames = padded.shape[0] - 2
    rows = padded.shape[1]
    inner = padded.shape[3]
    margin = 0 if edged else 1
    padded = jnp.pad(padded, ((0, 0), (1, 1), (margin, margin), (0, 0)))
    cols = padded.shape[2] - 2
    windows = []
    for step_t in range(3):
        for step_h in range(3):
            for step_w in range(3):
                windows.append(padded[step_t:step_t + frames, step_h:step_h + rows, step_w:step_w + cols, :])
    stacked = jnp.concatenate(windows, axis=-1).reshape(frames * rows * cols, 27 * inner)
    total = jnp.dot(stacked, weight.reshape(27 * inner, weight.shape[-1]), preferred_element_type=jnp.float32)
    return (total + bias).reshape(frames, rows, cols, weight.shape[-1])

def activate(hidden, gain):
    values = hidden.astype(jnp.float32)
    scale = jax.lax.rsqrt(lax.optimization_barrier(jnp.mean(values * values, axis=-1, keepdims=True)) + 1e-06)
    return jax.nn.silu(values * scale * gain).astype(jnp.bfloat16)

def reference(latent, w_in, b_in, gain, w_mid, b_mid, w_time, b_time):
    lat = latent.reshape(LF, H, W, ZC)
    zeros_in = jnp.zeros((2, H, W, ZC), latent.dtype)
    h0 = conv_input(jnp.concatenate([zeros_in, lat], axis=0), w_in, b_in, False).astype(jnp.bfloat16)
    act = activate(h0, gain)
    zeros_mid = jnp.zeros((2, H, W, C), jnp.bfloat16)
    h1 = (h0.astype(jnp.float32) + conv_valid(jnp.concatenate([zeros_mid, act], axis=0), w_mid, b_mid, True, False)).astype(jnp.bfloat16)
    up = conv_valid(jnp.concatenate([zeros_mid, h1], axis=0), w_time, b_time, False, False)
    paired = up.reshape(LF, H, W, 2, C).transpose(0, 3, 1, 2, 4)
    return paired.reshape(2 * LF, H, W, C).astype(jnp.bfloat16)
```

```python
import functools

import jax
import jax.numpy as jnp
from jax import lax
from jax.experimental import pallas as pl
from jax.experimental.pallas import tpu as pltpu
from jax.sharding import PartitionSpec as P

ZC = 16
C = 384
H = 16
W = 32
F = 2
KT = 64
ROW = W * ZC
WIDE = ROW + 128
MESH = pl.DeviceIdType.MESH
CHUNK = 16


def kernel(
    n, latent_ref, w_in_ref, b_in_ref, gain_ref, w_mid_ref, b_mid_ref, w_time_ref,
    part, halo, wtime,
    b_in, gain, b_mid, mine, padded, sent, got, spread, shifted, win, wmid, act_ref, hid, turn, own,
    lat_send, lat_recv, halo_send, halo_recv, win_sem, wmid_sem, wtime_sem, mine_sem, vec_sem,
):
    me = lax.axis_index("tm")
    block = latent_ref.shape[1]
    frames = latent_ref.shape[0]
    per_row = ROW // block

    mine_copy = pltpu.make_async_copy(latent_ref, mine, mine_sem)
    mine_copy.start()
    vectors = ((b_in_ref, b_in), (gain_ref, gain), (b_mid_ref, b_mid))
    vec_copies = [
        pltpu.make_async_copy(src, dst, vec_sem.at[v]) for v, (src, dst) in enumerate(vectors)
    ]
    for copy in vec_copies:
        copy.start()
    for t in range(9):
        pltpu.make_async_copy(w_in_ref.at[t], win.at[pl.ds(t * KT, 48)], win_sem.at[t]).start()
    mid_copies = [
        pltpu.make_async_copy(
            w_mid_ref.at[dt, di], wmid.at[dt, :, :, pl.ds(di * C, C)], wmid_sem.at[dt * 3 + di]
        )
        for dt in range(3)
        for di in range(3)
    ]
    for copy in mid_copies:
        copy.start()
    pltpu.make_async_copy(w_time_ref, wtime, wtime_sem).start()

    barrier = pltpu.get_barrier_semaphore()

    def greet(o, carry):
        pl.semaphore_signal(
            barrier, inc=1, device_id={"tm": lax.rem(me + o, n)}, device_id_type=MESH
        )
        return carry

    lax.fori_loop(1, n, greet, 0)

    padded[pl.ds(0, 8), :] = jnp.zeros((8, block), jnp.float32)
    padded[pl.ds(frames, 16), :] = jnp.zeros((16, block), jnp.float32)
    mine_copy.wait()
    padded[pl.ds(4, frames), :] = mine[...].astype(jnp.float32)
    for d in range(n):
        sent[d] = padded[pl.ds(F * d, 8), :].astype(jnp.bfloat16)

    for t in range(9):
        win[pl.ds(t * KT + 48, 16), :] = jnp.zeros((16, C), jnp.bfloat16)
    win[pl.ds(9 * KT, KT), :] = jnp.zeros((KT, C), jnp.bfloat16)
    act_ref[0] = jnp.zeros(act_ref.shape[1:], jnp.bfloat16)
    act_ref[W + 1] = jnp.zeros(act_ref.shape[1:], jnp.bfloat16)

    pl.semaphore_wait(barrier, n - 1)

    def lat_copy(o):
        d = lax.rem(me + o, n)
        return pltpu.make_async_remote_copy(
            src_ref=sent.at[d], dst_ref=got.at[me], send_sem=lat_send.at[d],
            recv_sem=lat_recv.at[me], device_id={"tm": d}, device_id_type=MESH,
        )

    def send(o, carry):
        lat_copy(o).start()
        return carry

    lax.fori_loop(1, n, send, 0)
    got[me] = sent[me]

    def receive(o, carry):
        j = lax.rem(me + o, n)
        pltpu.make_async_remote_copy(
            src_ref=sent.at[j], dst_ref=got.at[j], send_sem=lat_send.at[j],
            recv_sem=lat_recv.at[j], device_id={"tm": j}, device_id_type=MESH,
        ).wait_recv()
        return carry

    lax.fori_loop(1, n, receive, 0)

    flat = got[...].astype(jnp.float32).reshape(n * 8, block)
    for c in range(block // 128):
        spread[c] = flat[:, c * 128 : (c + 1) * 128]
    picked = []
    for s in range(F + 4):
        parts = [
            spread[c, pl.ds(b * 8 + s, H, stride=8 * per_row), :]
            for b in range(per_row)
            for c in range(block // 128)
        ]
        parts.append(jnp.zeros((H, 128), jnp.float32))
        picked.append(jnp.concatenate(parts, axis=1))
    lat = jnp.concatenate(picked, axis=0)
    total = (F + 4) * H
    row_of = lax.broadcasted_iota(jnp.int32, (total, WIDE), 0) & (H - 1)
    for di in range(3):
        if di == 0:
            moved = jnp.where(row_of == 0, 0.0, pltpu.roll(lat, 1, 0))
        elif di == 2:
            moved = jnp.where(row_of == H - 1, 0.0, pltpu.roll(lat, total - 1, 0))
        else:
            moved = lat
        shifted[0, di] = moved
        shifted[1, di] = pltpu.roll(moved, KT, 1)

    for t in range(9):
        pltpu.make_async_copy(w_in_ref.at[t], win.at[pl.ds(t * KT, 48)], win_sem.at[t]).wait()

    for copy in vec_copies:
        copy.wait()

    wide = (F + 2) * H
    rows = 4 * wide
    first = jnp.where(me > 0, 0, 2)

    def columns(k, carry):
        lane = lax.broadcasted_iota(jnp.int32, (wide, WIDE), 1)
        even = ((lane - ZC * (k - 1)) & 127) < KT
        turnby = lax.rem(WIDE + ZC - ZC * k, WIDE)
        pieces = []
        for p in range(5):
            dt, di = divmod(2 * p, 3)
            both = shifted[0, di, pl.ds(dt * H, wide), :]
            if p < 4:
                dt, di = divmod(2 * p + 1, 3)
                both = jnp.where(even, both, shifted[1, di, pl.ds(dt * H, wide), :])
            pieces.append(pltpu.roll(both, turnby, 1)[:, :ROW].astype(jnp.bfloat16))
        left = jnp.concatenate(
            [
                jnp.concatenate([piece[:, g * 128 : (g + 1) * 128] for piece in pieces], axis=1)
                for g in range(4)
            ],
            axis=0,
        )
        h0 = jnp.dot(left, win[...], preferred_element_type=jnp.float32) + b_in[...][None, :]
        h0 = h0.astype(jnp.bfloat16)
        values = h0.astype(jnp.float32)
        scale = lax.rsqrt(jnp.mean(values * values, axis=-1, keepdims=True) + 1e-06)
        v = values * scale * gain[...][None, :]
        half = 0.5 * v
        act = half + half * jnp.tanh(half)
        row = lax.broadcasted_iota(jnp.int32, (rows, C), 0)
        act = jnp.where(((row >> 4) & 3) >= first, act, 0.0)
        act = act.astype(jnp.bfloat16)
        for g in range(4):
            act_ref[pl.ds(g * 8 + k + 1, 1)] = act[g * wide : (g + 1) * wide].reshape(
                1, F + 2, H, C
            )
            for a in range(F):
                hid[g * 8 + k, a] = h0[g * wide + (a + 2) * H : g * wide + (a + 3) * H]
        return carry

    lax.fori_loop(0, 8, columns, 0)

    for copy in mid_copies:
        copy.wait()

    after = lax.rem(me + 1, n)

    def halo_copy(m):
        f = m // (W // CHUNK)
        w0 = pl.multiple_of(lax.rem(m, W // CHUNK) * CHUNK, CHUNK)
        return pltpu.make_async_remote_copy(
            src_ref=own.at[f, :, pl.ds(w0, CHUNK)], dst_ref=halo.at[f, :, pl.ds(w0, CHUNK)],
            send_sem=halo_send.at[m], recv_sem=halo_recv.at[m],
            device_id={"tm": after}, device_id_type=MESH,
        )

    def residual(m, carry):
        f = m // (W // CHUNK)
        w0 = pl.multiple_of(lax.rem(m, W // CHUNK) * CHUNK, CHUNK)
        left = jnp.concatenate(
            [
                act_ref[pl.ds(w0 + dj, CHUNK), f + dt].reshape(CHUNK * H, C)
                for dt in range(3)
                for dj in range(3)
            ],
            axis=1,
        )
        three = jnp.dot(
            left, wmid[...].reshape(9 * C, 3 * C), preferred_element_type=jnp.float32
        )
        row = lax.broadcasted_iota(jnp.int32, (CHUNK * H, C), 0) & (H - 1)
        above = pltpu.roll(three[:, :C], 1, 0)
        below = pltpu.roll(three[:, 2 * C :], CHUNK * H - 1, 0)
        acc = hid[pl.ds(w0, CHUNK), f].astype(jnp.float32).reshape(CHUNK * H, C)
        acc = acc + b_mid[...][None, :] + three[:, C : 2 * C]
        acc = acc + jnp.where(row == 0, 0.0, above) + jnp.where(row == H - 1, 0.0, below)
        for c in range(C // 128):
            turn[c] = acc[:, c * 128 : (c + 1) * 128]
        for i in range(H):
            line = [turn[c, pl.ds(i, CHUNK, stride=H), :] for c in range(C // 128)]
            own[f, i, pl.ds(w0, CHUNK)] = jnp.concatenate(line, axis=1).astype(jnp.bfloat16)

        @pl.when(me < n - 1)
        def _():
            halo_copy(m).start()

        return carry

    chunks = F * (W // CHUNK)
    lax.fori_loop(0, chunks, residual, 0)

    pltpu.make_async_copy(w_time_ref, wtime, wtime_sem).wait()

    def upsample_own(q, carry):
        mine0, mine1 = (own[f, pl.ds(q * 4, 4)].reshape(4 * W, C) for f in range(F))
        here = pl.ds(q * 4 * W, 4 * W)
        part[0, here] = jnp.dot(
            mine0, wtime[pl.ds(2 * C, C)], preferred_element_type=jnp.float32
        )
        part[1, here] = jnp.dot(
            jnp.concatenate([mine0, mine1], axis=1),
            wtime[pl.ds(C, 2 * C)],
            preferred_element_type=jnp.float32,
        )
        return carry

    lax.fori_loop(0, H // 4, upsample_own, 0)

    @pl.when(me > 0)
    def _():
        for m in range(chunks):
            halo_copy(m).wait_recv()

    @pl.when(me == 0)
    def _():
        halo[...] = jnp.zeros(halo.shape, jnp.bfloat16)

    def sent_all(o, carry):
        lat_copy(o).wait_send()
        return carry

    lax.fori_loop(1, n, sent_all, 0)

    @pl.when(me < n - 1)
    def _():
        for m in range(chunks):
            halo_copy(m).wait_send()


def finish(part, halo, wtime, b_time, out_ref, staged, out_sem):
    rows = 4

    def out_copy(q, e):
        return pltpu.make_async_copy(
            staged.at[e, pl.ds(q * rows, rows)], out_ref.at[e, pl.ds(q * rows, rows)],
            out_sem.at[q, e],
        )

    for q in range(H // rows):
        i0 = q * rows
        past0, past1 = (halo[f, pl.ds(i0, rows)].reshape(rows * W, C) for f in range(F))
        here = pl.ds(i0 * W, rows * W)
        from_halo = (
            jnp.dot(
                jnp.concatenate([past0, past1], axis=1),
                wtime[pl.ds(0, 2 * C)],
                preferred_element_type=jnp.float32,
            ),
            jnp.dot(past1, wtime[pl.ds(0, C)], preferred_element_type=jnp.float32),
        )
        for f in range(F):
            up = from_halo[f] + part[f, here] + b_time[...][None, :]
            up = up.astype(jnp.bfloat16)
            for s in range(2):
                staged[2 * f + s, pl.ds(i0, rows)] = up[:, s * C : (s + 1) * C].reshape(rows, W, C)
        for e in range(2 * F):
            out_copy(q, e).start()
    for q in range(H // rows):
        for e in range(2 * F):
            out_copy(q, e).wait()


def per_device(n, latent, w_in, b_in, gain, w_mid, b_mid, w_time, b_time):
    frames, block = latent.shape
    assert frames == F * n
    bf16, f32 = jnp.bfloat16, jnp.float32
    vmem = pl.BlockSpec(memory_space=pltpu.VMEM)
    hbm = pl.BlockSpec(memory_space=pltpu.HBM)
    chunks = F * (W // CHUNK)
    dma = pltpu.SemaphoreType.DMA
    part, halo, wtime = pl.pallas_call(
        functools.partial(kernel, n),
        out_shape=(
            pltpu.VMEM((F, H * W, 2 * C), f32),
            pltpu.VMEM((F, H, W, C), bf16),
            pltpu.VMEM((3 * C, 2 * C), bf16),
        ),
        in_specs=[hbm] * 7,
        out_specs=[vmem] * 3,
        scratch_shapes=[
            pltpu.VMEM((C,), f32), pltpu.VMEM((C,), f32), pltpu.VMEM((C,), f32),
            pltpu.VMEM((frames, block), bf16),
            pltpu.VMEM((frames + 16, block), f32),
            pltpu.VMEM((n, 8, block), bf16),
            pltpu.VMEM((n, 8, block), bf16),
            pltpu.VMEM((block // 128, n * 8, 128), f32),
            pltpu.VMEM((2, 3, (F + 4) * H, WIDE), f32),
            pltpu.VMEM((10 * KT, C), bf16),
            pltpu.VMEM((3, 3, C, 3 * C), bf16),
            pltpu.VMEM((W + 2, F + 2, H, C), bf16),
            pltpu.VMEM((W, F, H, C), bf16),
            pltpu.VMEM((C // 128, CHUNK * H, 128), f32),
            pltpu.VMEM((F, H, W, C), bf16),
            dma((n,)), dma((n,)), dma((chunks,)), dma((chunks,)), dma((9,)), dma((9,)), dma(()), dma(()), dma((3,)),
        ],
        compiler_params=pltpu.CompilerParams(
            collective_id=0, has_side_effects=True, vmem_limit_bytes=44000000
        ),
        name="decoder_window",
    )(
        *(
            pltpu.with_memory_space_constraint(x, pltpu.HBM)
            for x in (
                latent, w_in.reshape(9, 3 * ZC, C), b_in, gain, w_mid, b_mid,
                w_time.reshape(3 * C, 2 * C),
            )
        )
    )
    part, halo, wtime = (
        pltpu.with_memory_space_constraint(x, pltpu.VMEM) for x in (part, halo, wtime)
    )
    return pl.pallas_call(
        finish,
        out_shape=jax.ShapeDtypeStruct((2 * F, H, W, C), bf16),
        in_specs=[vmem] * 4,
        out_specs=hbm,
        scratch_shapes=[pltpu.VMEM((2 * F, H, W, C), bf16), dma((4, 2 * F))],
        compiler_params=pltpu.CompilerParams(vmem_limit_bytes=44000000),
        name="finish",
    )(part, halo, wtime, b_time)


def solution(mesh):
    n = mesh.shape["tm"]
    return jax.shard_map(
        functools.partial(per_device, n),
        mesh=mesh,
        in_specs=(P("groups", "tm"), P(), P(), P(), P(), P(), P(), P()),
        out_specs=P(("groups", "tm"), None, None, None),
        check_vma=False,
    )
```

```python
import functools

import jax
import jax.numpy as jnp
from jax import lax
from jax.experimental import pallas as pl
from jax.experimental.pallas import tpu as pltpu
from jax.sharding import PartitionSpec as P

ZC = 16
C = 384
H = 16
W = 32
F = 2
ROW = W * ZC
WIDE = ROW + 128
GROUP = 4
HALF = W // 2
PARTS = ((0, 256), (256, 128))
MESH = pl.DeviceIdType.MESH


def kernel(
    n, latent_ref, w_in_ref, b_in_ref, gain_ref, w_mid_ref, b_mid_ref, w_time_ref,
    part, halo_a, halo_b, wtime,
    b_in, gain, b_mid, mine, padded, sent, got, spread, rolled, win, band, wmid, mixed, hid, product, turn, own_a, own_b,
    lat_send, lat_recv, halo_send, halo_recv, win_sem, wmid_sem, wtime_sem, mine_sem, vec_sem,
):
    bf16, f32 = jnp.bfloat16, jnp.float32
    me = lax.axis_index("tm")
    block = latent_ref.shape[1]
    frames = latent_ref.shape[0]
    per_row = ROW // block

    mine_copy = pltpu.make_async_copy(latent_ref, mine, mine_sem)
    mine_copy.start()

    win_copy = pltpu.make_async_copy(w_in_ref, win, win_sem)
    vectors = ((b_in_ref, b_in), (gain_ref, gain), (b_mid_ref, b_mid))
    vec_copies = [
        pltpu.make_async_copy(src, dst, vec_sem.at[v]) for v, (src, dst) in enumerate(vectors)
    ]
    mid_copies = [
        [
            pltpu.make_async_copy(
                w_mid_ref.at[dt, di], wmid.at[(0, 1, 3)[dt], di], wmid_sem.at[di * 3 + dt]
            )
            for dt in range(3)
        ]
        for di in range(3)
    ]
    wtime_copy = pltpu.make_async_copy(w_time_ref, wtime, wtime_sem)

    def fetch():
        win_copy.start()
        for copy in vec_copies:
            copy.start()
        for copies in mid_copies:
            for copy in copies:
                copy.start()
        wtime_copy.start()

    @pl.when(me < n // 2)
    def _():
        fetch()

    barrier = pltpu.get_barrier_semaphore()

    def greet(d, carry):
        pl.semaphore_signal(barrier, inc=1, device_id={"tm": d}, device_id_type=MESH)
        return carry

    lax.fori_loop(me + 1, n, greet, 0)

    padded[pl.ds(0, 8), :] = jnp.zeros((8, block), f32)
    padded[pl.ds(frames, 16), :] = jnp.zeros((16, block), f32)
    mine_copy.wait()
    padded[pl.ds(4, frames), :] = mine[...].astype(f32)
    for d in range(n):
        sent[d] = padded[pl.ds(F * d, 8), :].astype(bf16)

    @pl.when(me > 0)
    def _():
        pl.semaphore_wait(barrier, me)

    def lat_copy(d, j):
        return pltpu.make_async_remote_copy(
            src_ref=sent.at[d], dst_ref=got.at[j], send_sem=lat_send.at[d],
            recv_sem=lat_recv.at[j], device_id={"tm": d}, device_id_type=MESH,
        )

    def send(d, carry):
        lat_copy(d, me).start()
        return carry

    lax.fori_loop(0, me, send, 0)

    @pl.when(me >= n // 2)
    def _():
        fetch()

    def clear(t, carry):
        band[pl.ds(t * 128, 128), :] = jnp.zeros((128, GROUP * C), bf16)
        return carry

    lax.fori_loop(0, 9, clear, 0)
    for m in range(4):
        mixed[m, 0] = jnp.zeros((H, C), bf16)
        mixed[m, W + 1] = jnp.zeros((H, C), bf16)
    got[me] = sent[me]
    win_copy.wait()
    for t in range(9):
        for c in range(GROUP):
            band[pl.ds(t * 128 + ZC * c, 3 * ZC), pl.ds(c * C, C)] = win[t]
    for copy in vec_copies:
        copy.wait()

    def answer(o, carry):
        d = n - 1 - o
        lat_copy(d, d).wait_recv()
        lat_copy(d, me).start()
        return carry

    for di, copies in enumerate(mid_copies):
        if di == 2:
            lax.fori_loop(0, n - 1 - me, answer, 0)
        for copy in copies:
            copy.wait()

        def combine(q, carry, di=di):
            here = (di, pl.ds(pl.multiple_of(q * 64, 64), 64))
            outer = wmid[0, *here].astype(f32) + wmid[3, *here].astype(f32)
            inner = wmid[1, *here].astype(f32)
            wmid[1, *here] = (outer + inner).astype(bf16)
            wmid[2, *here] = (outer - inner).astype(bf16)
            return carry

        lax.fori_loop(0, 3 * C // 64, combine, 0)
    if False:
        lax.fori_loop(0, n - 1 - me, answer, 0)

    def receive(d, carry):
        lat_copy(d, d).wait_recv()
        return carry

    lax.fori_loop(0, me, receive, 0)

    flat = got[...].astype(f32).reshape(n * 8, block)
    for c in range(block // 128):
        spread[c] = flat[:, c * 128 : (c + 1) * 128]
    picked = []
    for s in range(F + 4):
        parts = [
            spread[c, pl.ds(b * 8 + s, H, stride=8 * per_row), :]
            for b in range(per_row)
            for c in range(block // 128)
        ]
        parts.append(jnp.zeros((H, 128), f32))
        picked.append(jnp.concatenate(parts, axis=1))
    lat = jnp.concatenate(picked, axis=0)
    total = (F + 4) * H
    row_of = lax.broadcasted_iota(jnp.int32, (total, ROW), 0) & (H - 1)
    for r in range(2):
        turned = pltpu.roll(lat, (ZC, WIDE - 3 * ZC)[r], 1)[:, :ROW]
        for di in range(3):
            if di == 0:
                moved = jnp.where(row_of == 0, 0.0, pltpu.roll(turned, 1, 0))
            elif di == 2:
                moved = jnp.where(row_of == H - 1, 0.0, pltpu.roll(turned, total - 1, 0))
            else:
                moved = turned
            rolled[r, di] = moved.astype(bf16)

    wide = (F + 2) * H
    keep = jnp.where(me > 0, 1.0, 0.0)

    def columns(r, carry):
        left = jnp.concatenate(
            [
                jnp.concatenate(
                    [
                        rolled[r, t % 3, pl.ds((t // 3) * H, wide), pl.ds(128 * b, 128)]
                        for b in range(4)
                    ],
                    axis=0,
                )
                for t in range(9)
            ],
            axis=1,
        )
        for pair in range(2):
            both = jnp.dot(
                left, band[:, pl.ds(pair * 2 * C, 2 * C)], preferred_element_type=f32
            )
            for c in range(2):
                h0 = (both[:, c * C : (c + 1) * C] + b_in[...][None, :]).astype(bf16)
                values = h0.astype(f32)
                scale = lax.rsqrt(jnp.mean(values * values, axis=-1, keepdims=True) + 1e-06)
                half = values * (0.5 * scale) * gain[...][None, :]
                act = half + half * jnp.tanh(half)
                for b in range(4):
                    w = 8 * b + 4 * r + 2 * pair + c
                    d0, d1, d2, d3 = (
                        act[b * wide + f * H : b * wide + (f + 1) * H] for f in range(4)
                    )
                    d0, d1 = d0 * keep, d1 * keep
                    mixed[0, w + 1] = (d0 - d2).astype(bf16)
                    mixed[1, w + 1] = (0.5 * (d1 + d2)).astype(bf16)
                    mixed[2, w + 1] = (0.5 * (d2 - d1)).astype(bf16)
                    mixed[3, w + 1] = (d1 - d3).astype(bf16)
                    for a in range(F):
                        hid[w, a] = h0[b * wide + (a + 2) * H : b * wide + (a + 3) * H]
        return carry

    lax.fori_loop(0, 2, columns, 0)

    after = lax.rem(me + 1, n)

    own, halo = (own_a, own_b), (halo_a, halo_b)

    def halo_copy(h, p):
        return pltpu.make_async_remote_copy(
            src_ref=own[p].at[h], dst_ref=halo[p].at[h],
            send_sem=halo_send.at[h * 2 + p], recv_sem=halo_recv.at[h * 2 + p],
            device_id={"tm": after}, device_id_type=MESH,
        )

    rows = HALF * H

    def residual(h, carry):
        w0 = pl.multiple_of(h * HALF, HALF)
        for p, (c0, width) in enumerate(PARTS):
            for m in range(4):
                left = jnp.concatenate(
                    [mixed[m, pl.ds(w0 + dj, HALF)].reshape(rows, C) for dj in range(3)], axis=1
                )
                product[m, :, pl.ds(0, 3 * width)] = jnp.dot(
                    left,
                    jnp.concatenate(
                        [wmid[m, di, :, pl.ds(c0, width)] for di in range(3)], axis=1
                    ),
                    preferred_element_type=f32,
                )
            p0, p1, p2, p3 = (product[m, :, pl.ds(0, 3 * width)] for m in range(4))
            row = lax.broadcasted_iota(jnp.int32, (rows, width), 0) & (H - 1)
            for f, three in enumerate((p0 + p1 + p2, p1 - p2 - p3)):
                above = pltpu.roll(three[:, :width], 1, 0)
                below = pltpu.roll(three[:, 2 * width :], rows - 1, 0)
                acc = hid[pl.ds(w0, HALF), f, :, pl.ds(c0, width)].astype(f32).reshape(rows, width)
                acc = acc + b_mid[pl.ds(c0, width)][None, :] + three[:, width : 2 * width]
                acc = acc + jnp.where(row == 0, 0.0, above) + jnp.where(row == H - 1, 0.0, below)
                for c in range(width // 128):
                    turn[f * 2 + c] = acc[:, c * 128 : (c + 1) * 128]
                for i in range(H):
                    line = [
                        turn[f * 2 + c, pl.ds(i, HALF, stride=H), :] for c in range(width // 128)
                    ]
                    own[p][h, f, i] = jnp.concatenate(
                        line, axis=1
                    ).astype(bf16)

            @pl.when(me < n - 1)
            def _():
                halo_copy(h, p).start()

        return carry

    lax.fori_loop(0, 2, residual, 0)

    wtime_copy.wait()

    def both(pair, h, f):
        return jnp.concatenate(
            [ref[h, f].reshape(rows, width) for ref, (_, width) in zip(pair, PARTS)], axis=1
        )

    for h in range(2):
        mine0, mine1 = (both(own, h, f) for f in range(F))
        part[0, h] = jnp.dot(mine0, wtime[pl.ds(2 * C, C)], preferred_element_type=f32)
        part[1, h] = jnp.dot(
            jnp.concatenate([mine0, mine1], axis=1), wtime[pl.ds(C, 2 * C)],
            preferred_element_type=f32,
        )

    @pl.when(me > 0)
    def _():
        for p in range(2):
            halo_copy(0, p).wait_recv()

    @pl.when(me == 0)
    def _():
        for ref in halo:
            ref[...] = jnp.zeros(ref.shape, bf16)

    past0, past1 = (both(halo, 0, f) for f in range(F))
    part[0, 0] += jnp.dot(
        jnp.concatenate([past0, past1], axis=1), wtime[pl.ds(0, 2 * C)],
        preferred_element_type=f32,
    )
    part[1, 0] += jnp.dot(past1, wtime[pl.ds(0, C)], preferred_element_type=f32)

    @pl.when(me > 0)
    def _():
        for p in range(2):
            halo_copy(1, p).wait_recv()

    def sent_all(d, carry):
        lat_copy(d, me).wait_send()
        return carry

    lax.fori_loop(0, me, sent_all, 0)
    lax.fori_loop(me + 1, n, sent_all, 0)

    @pl.when(me < n - 1)
    def _():
        for h in range(2):
            for p in range(2):
                halo_copy(h, p).wait_send()


def finish(part, halo_a, halo_b, wtime, b_time, out_ref, staged, out_sem):
    rows = HALF * H

    def out_copy(h, e):
        return pltpu.make_async_copy(
            staged.at[h, e], out_ref.at[e, :, pl.ds(h * HALF, HALF)], out_sem.at[h, e]
        )

    def put(h, f, up):
        up = (up + b_time[...][None, :]).astype(jnp.bfloat16)
        for s in range(2):
            staged[h, 2 * f + s] = up[:, s * C : (s + 1) * C].reshape(H, HALF, C)
            out_copy(h, 2 * f + s).start()

    for f in range(F):
        put(0, f, part[f, 0])
    past0, past1 = (
        jnp.concatenate(
            [halo_a[1, f].reshape(rows, 256), halo_b[1, f].reshape(rows, 128)], axis=1
        )
        for f in range(F)
    )
    put(1, 1, part[1, 1] + jnp.dot(past1, wtime[pl.ds(0, C)], preferred_element_type=jnp.float32))
    put(
        1, 0,
        part[0, 1]
        + jnp.dot(
            jnp.concatenate([past0, past1], axis=1), wtime[pl.ds(0, 2 * C)],
            preferred_element_type=jnp.float32,
        ),
    )
    for h in range(2):
        for e in range(2 * F):
            out_copy(h, e).wait()


def per_device(n, latent, w_in, b_in, gain, w_mid, b_mid, w_time, b_time):
    frames, block = latent.shape
    assert frames == F * n
    bf16, f32 = jnp.bfloat16, jnp.float32
    vmem = pl.BlockSpec(memory_space=pltpu.VMEM)
    hbm = pl.BlockSpec(memory_space=pltpu.HBM)
    dma = pltpu.SemaphoreType.DMA
    handed = pl.pallas_call(
        functools.partial(kernel, n),
        out_shape=(
            pltpu.VMEM((F, 2, HALF * H, 2 * C), f32),
            pltpu.VMEM((2, F, H, HALF, 256), bf16),
            pltpu.VMEM((2, F, H, HALF, 128), bf16),
            pltpu.VMEM((3 * C, 2 * C), bf16),
        ),
        in_specs=[hbm] * 7,
        out_specs=[vmem] * 4,
        scratch_shapes=[
            pltpu.VMEM((C,), f32), pltpu.VMEM((C,), f32), pltpu.VMEM((C,), f32),
            pltpu.VMEM((frames, block), bf16),
            pltpu.VMEM((frames + 16, block), f32),
            pltpu.VMEM((n, 8, block), bf16),
            pltpu.VMEM((n, 8, block), bf16),
            pltpu.VMEM((block // 128, n * 8, 128), f32),
            pltpu.VMEM((2, 3, (F + 4) * H, ROW), bf16),
            pltpu.VMEM((9, 3 * ZC, C), bf16),
            pltpu.VMEM((9 * 128, GROUP * C), bf16),
            pltpu.VMEM((4, 3, 3 * C, C), bf16),
            pltpu.VMEM((4, W + 2, H, C), bf16),
            pltpu.VMEM((W, F, H, C), bf16),
            pltpu.VMEM((4, HALF * H, 3 * 256), f32),
            pltpu.VMEM((4, HALF * H, 128), f32),
            pltpu.VMEM((2, F, H, HALF, 256), bf16), pltpu.VMEM((2, F, H, HALF, 128), bf16),
            dma((n,)), dma((n,)), dma((4,)), dma((4,)), dma(()), dma((9,)), dma(()), dma(()), dma((3,)),
        ],
        compiler_params=pltpu.CompilerParams(
            collective_id=0, has_side_effects=True, vmem_limit_bytes=44000000
        ),
        name="decoder_window",
    )(
        *(
            pltpu.with_memory_space_constraint(x, pltpu.HBM)
            for x in (
                latent, w_in.reshape(9, 3 * ZC, C), b_in, gain, w_mid.reshape(3, 3, 3 * C, C), b_mid,
                w_time.reshape(3 * C, 2 * C),
            )
        )
    )
    handed = [pltpu.with_memory_space_constraint(x, pltpu.VMEM) for x in handed]
    return pl.pallas_call(
        finish,
        out_shape=jax.ShapeDtypeStruct((2 * F, H, W, C), bf16),
        in_specs=[vmem] * 5,
        out_specs=hbm,
        scratch_shapes=[pltpu.VMEM((2, 2 * F, H, HALF, C), bf16), dma((2, 2 * F))],
        compiler_params=pltpu.CompilerParams(vmem_limit_bytes=44000000),
        name="finish",
    )(*handed, b_time)


def solution(mesh):
    n = mesh.shape["tm"]
    return jax.shard_map(
        functools.partial(per_device, n),
        mesh=mesh,
        in_specs=(P("groups", "tm"), P(), P(), P(), P(), P(), P(), P()),
        out_specs=P(("groups", "tm"), None, None, None),
        check_vma=False,
    )
```

```python
import functools

import jax
import jax.numpy as jnp
from jax import lax
from jax.experimental import pallas as pl
from jax.experimental.pallas import tpu as pltpu
from jax.sharding import PartitionSpec as P

ZC = 16
C = 384
H = 16
W = 32
F = 2
ROW = W * ZC
WIDE = ROW + 128
GROUP = 4
HALF = W // 2
PARTS = ((0, 256), (256, 128))
MESH = pl.DeviceIdType.MESH


def kernel(
    n, latent_ref, w_in_ref, b_in_ref, gain_ref, w_mid_ref, b_mid_ref, w_time_ref,
    part, halo_a, halo_b, wtime,
    b_in, gain, b_mid, mine, padded, sent, got, spread, rolled, win, band, wmid, mixed, hid, product, turn, own_a, own_b,
    lat_send, lat_recv, halo_send, halo_recv, win_sem, wmid_sem, wtime_sem, mine_sem, vec_sem,
):
    bf16, f32 = jnp.bfloat16, jnp.float32
    me = lax.axis_index("tm")
    block = latent_ref.shape[1]
    frames = latent_ref.shape[0]
    per_row = ROW // block

    mine_copy = pltpu.make_async_copy(latent_ref, mine, mine_sem)
    mine_copy.start()

    win_copy = pltpu.make_async_copy(w_in_ref, win, win_sem)
    vectors = ((b_in_ref, b_in), (gain_ref, gain), (b_mid_ref, b_mid))
    vec_copies = [
        pltpu.make_async_copy(src, dst, vec_sem.at[v]) for v, (src, dst) in enumerate(vectors)
    ]
    mid_copies = [
        [
            pltpu.make_async_copy(
                w_mid_ref.at[dt, di], wmid.at[(0, 1, 3)[dt], di], wmid_sem.at[di * 3 + dt]
            )
            for dt in range(3)
        ]
        for di in range(3)
    ]
    wtime_copy = pltpu.make_async_copy(w_time_ref, wtime, wtime_sem)

    def fetch():
        win_copy.start()
        for copy in vec_copies:
            copy.start()
        for copies in mid_copies:
            for copy in copies:
                copy.start()
        wtime_copy.start()

    @pl.when(me < n // 2)
    def _():
        fetch()

    barrier = pltpu.get_barrier_semaphore()

    def other(o):
        return lax.rem(me + o, n)

    def greet(o, carry):
        pl.semaphore_signal(barrier, inc=1, device_id={"tm": other(o)}, device_id_type=MESH)
        return carry

    lax.fori_loop(1, n, greet, 0)

    padded[pl.ds(0, 8), :] = jnp.zeros((8, block), f32)
    padded[pl.ds(frames, 16), :] = jnp.zeros((16, block), f32)
    mine_copy.wait()
    padded[pl.ds(4, frames), :] = mine[...].astype(f32)
    for d in range(n):
        sent[d] = padded[pl.ds(F * d, 8), :].astype(bf16)

    pl.semaphore_wait(barrier, n - 1)

    def lat_copy(d, j):
        return pltpu.make_async_remote_copy(
            src_ref=sent.at[d], dst_ref=got.at[j], send_sem=lat_send.at[d],
            recv_sem=lat_recv.at[j], device_id={"tm": d}, device_id_type=MESH,
        )

    def send(o, carry):
        lat_copy(other(o), me).start()
        return carry

    lax.fori_loop(1, n, send, 0)

    @pl.when(me >= n // 2)
    def _():
        fetch()

    def clear(t, carry):
        band[pl.ds(t * 128, 128), :] = jnp.zeros((128, GROUP * C), bf16)
        return carry

    lax.fori_loop(0, 9, clear, 0)
    for m in range(4):
        mixed[m, 0] = jnp.zeros((H, C), bf16)
        mixed[m, W + 1] = jnp.zeros((H, C), bf16)
    got[me] = sent[me]
    win_copy.wait()
    for t in range(9):
        for c in range(GROUP):
            band[pl.ds(t * 128 + ZC * c, 3 * ZC), pl.ds(c * C, C)] = win[t]
    for copy in vec_copies:
        copy.wait()

    for di, copies in enumerate(mid_copies):
        for copy in copies:
            copy.wait()

        def combine(q, carry, di=di):
            here = (di, pl.ds(pl.multiple_of(q * 64, 64), 64))
            outer = wmid[0, *here].astype(f32) + wmid[3, *here].astype(f32)
            inner = wmid[1, *here].astype(f32)
            wmid[1, *here] = (outer + inner).astype(bf16)
            wmid[2, *here] = (outer - inner).astype(bf16)
            return carry

        lax.fori_loop(0, 3 * C // 64, combine, 0)
    def receive(o, carry):
        lat_copy(other(o), other(o)).wait_recv()
        return carry

    lax.fori_loop(1, n, receive, 0)

    flat = got[...].astype(f32).reshape(n * 8, block)
    for c in range(block // 128):
        spread[c] = flat[:, c * 128 : (c + 1) * 128]
    picked = []
    for s in range(F + 4):
        parts = [
            spread[c, pl.ds(b * 8 + s, H, stride=8 * per_row), :]
            for b in range(per_row)
            for c in range(block // 128)
        ]
        parts.append(jnp.zeros((H, 128), f32))
        picked.append(jnp.concatenate(parts, axis=1))
    lat = jnp.concatenate(picked, axis=0)
    total = (F + 4) * H
    row_of = lax.broadcasted_iota(jnp.int32, (total, ROW), 0) & (H - 1)
    for r in range(2):
        turned = pltpu.roll(lat, (ZC, WIDE - 3 * ZC)[r], 1)[:, :ROW]
        for di in range(3):
            if di == 0:
                moved = jnp.where(row_of == 0, 0.0, pltpu.roll(turned, 1, 0))
            elif di == 2:
                moved = jnp.where(row_of == H - 1, 0.0, pltpu.roll(turned, total - 1, 0))
            else:
                moved = turned
            rolled[r, di] = moved.astype(bf16)

    wide = (F + 2) * H
    keep = jnp.where(me > 0, 1.0, 0.0)

    def columns(r, carry):
        left = jnp.concatenate(
            [
                jnp.concatenate(
                    [
                        rolled[r, t % 3, pl.ds((t // 3) * H, wide), pl.ds(128 * b, 128)]
                        for b in range(4)
                    ],
                    axis=0,
                )
                for t in range(9)
            ],
            axis=1,
        )
        for pair in range(2):
            both = jnp.dot(
                left, band[:, pl.ds(pair * 2 * C, 2 * C)], preferred_element_type=f32
            )
            for c in range(2):
                h0 = (both[:, c * C : (c + 1) * C] + b_in[...][None, :]).astype(bf16)
                values = h0.astype(f32)
                scale = lax.rsqrt(jnp.mean(values * values, axis=-1, keepdims=True) + 1e-06)
                half = values * (0.5 * scale) * gain[...][None, :]
                act = half + half * jnp.tanh(half)
                for b in range(4):
                    w = 8 * b + 4 * r + 2 * pair + c
                    d0, d1, d2, d3 = (
                        act[b * wide + f * H : b * wide + (f + 1) * H] for f in range(4)
                    )
                    d0, d1 = d0 * keep, d1 * keep
                    mixed[0, w + 1] = (d0 - d2).astype(bf16)
                    mixed[1, w + 1] = (0.5 * (d1 + d2)).astype(bf16)
                    mixed[2, w + 1] = (0.5 * (d2 - d1)).astype(bf16)
                    mixed[3, w + 1] = (d1 - d3).astype(bf16)
                    for a in range(F):
                        hid[w, a] = h0[b * wide + (a + 2) * H : b * wide + (a + 3) * H]
        return carry

    lax.fori_loop(0, 2, columns, 0)

    after = lax.rem(me + 1, n)

    own, halo = (own_a, own_b), (halo_a, halo_b)

    def halo_copy(h, p):
        return pltpu.make_async_remote_copy(
            src_ref=own[p].at[h], dst_ref=halo[p].at[h],
            send_sem=halo_send.at[h * 2 + p], recv_sem=halo_recv.at[h * 2 + p],
            device_id={"tm": after}, device_id_type=MESH,
        )

    rows = HALF * H

    def residual(h, carry):
        w0 = pl.multiple_of(h * HALF, HALF)
        for p, (c0, width) in enumerate(PARTS):
            for m in range(4):
                left = jnp.concatenate(
                    [mixed[m, pl.ds(w0 + dj, HALF)].reshape(rows, C) for dj in range(3)], axis=1
                )
                product[m, :, pl.ds(0, 3 * width)] = jnp.dot(
                    left,
                    jnp.concatenate(
                        [wmid[m, di, :, pl.ds(c0, width)] for di in range(3)], axis=1
                    ),
                    preferred_element_type=f32,
                )
            p0, p1, p2, p3 = (product[m, :, pl.ds(0, 3 * width)] for m in range(4))
            row = lax.broadcasted_iota(jnp.int32, (rows, width), 0) & (H - 1)
            for f, three in enumerate((p0 + p1 + p2, p1 - p2 - p3)):
                above = pltpu.roll(three[:, :width], 1, 0)
                below = pltpu.roll(three[:, 2 * width :], rows - 1, 0)
                acc = hid[pl.ds(w0, HALF), f, :, pl.ds(c0, width)].astype(f32).reshape(rows, width)
                acc = acc + b_mid[pl.ds(c0, width)][None, :] + three[:, width : 2 * width]
                acc = acc + jnp.where(row == 0, 0.0, above) + jnp.where(row == H - 1, 0.0, below)
                for c in range(width // 128):
                    turn[f * 2 + c] = acc[:, c * 128 : (c + 1) * 128]
                for i in range(H):
                    line = [
                        turn[f * 2 + c, pl.ds(i, HALF, stride=H), :] for c in range(width // 128)
                    ]
                    own[p][h, f, i] = jnp.concatenate(
                        line, axis=1
                    ).astype(bf16)

            @pl.when(me < n - 1)
            def _():
                halo_copy(h, p).start()

        return carry

    lax.fori_loop(0, 2, residual, 0)

    wtime_copy.wait()

    def both(pair, h, f):
        return jnp.concatenate(
            [ref[h, f].reshape(rows, width) for ref, (_, width) in zip(pair, PARTS)], axis=1
        )

    for h in range(2):
        mine0, mine1 = (both(own, h, f) for f in range(F))
        part[0, h] = jnp.dot(mine0, wtime[pl.ds(2 * C, C)], preferred_element_type=f32)
        part[1, h] = jnp.dot(
            jnp.concatenate([mine0, mine1], axis=1), wtime[pl.ds(C, 2 * C)],
            preferred_element_type=f32,
        )

    @pl.when(me > 0)
    def _():
        for p in range(2):
            halo_copy(0, p).wait_recv()

    @pl.when(me == 0)
    def _():
        for ref in halo:
            ref[...] = jnp.zeros(ref.shape, bf16)

    past0, past1 = (both(halo, 0, f) for f in range(F))
    part[0, 0] += jnp.dot(
        jnp.concatenate([past0, past1], axis=1), wtime[pl.ds(0, 2 * C)],
        preferred_element_type=f32,
    )
    part[1, 0] += jnp.dot(past1, wtime[pl.ds(0, C)], preferred_element_type=f32)

    @pl.when(me > 0)
    def _():
        for p in range(2):
            halo_copy(1, p).wait_recv()

    def sent_all(o, carry):
        lat_copy(other(o), me).wait_send()
        return carry

    lax.fori_loop(1, n, sent_all, 0)

    @pl.when(me < n - 1)
    def _():
        for h in range(2):
            for p in range(2):
                halo_copy(h, p).wait_send()


def finish(part, halo_a, halo_b, wtime, b_time, out_ref, staged, out_sem):
    rows = HALF * H

    def out_copy(h, e):
        return pltpu.make_async_copy(
            staged.at[h, e], out_ref.at[e, :, pl.ds(h * HALF, HALF)], out_sem.at[h, e]
        )

    def put(h, f, up):
        up = (up + b_time[...][None, :]).astype(jnp.bfloat16)
        for s in range(2):
            staged[h, 2 * f + s] = up[:, s * C : (s + 1) * C].reshape(H, HALF, C)
            out_copy(h, 2 * f + s).start()

    for f in range(F):
        put(0, f, part[f, 0])
    past0, past1 = (
        jnp.concatenate(
            [halo_a[1, f].reshape(rows, 256), halo_b[1, f].reshape(rows, 128)], axis=1
        )
        for f in range(F)
    )
    put(1, 1, part[1, 1] + jnp.dot(past1, wtime[pl.ds(0, C)], preferred_element_type=jnp.float32))
    put(
        1, 0,
        part[0, 1]
        + jnp.dot(
            jnp.concatenate([past0, past1], axis=1), wtime[pl.ds(0, 2 * C)],
            preferred_element_type=jnp.float32,
        ),
    )
    for h in range(2):
        for e in range(2 * F):
            out_copy(h, e).wait()


def per_device(n, latent, w_in, b_in, gain, w_mid, b_mid, w_time, b_time):
    frames, block = latent.shape
    assert frames == F * n
    bf16, f32 = jnp.bfloat16, jnp.float32
    vmem = pl.BlockSpec(memory_space=pltpu.VMEM)
    hbm = pl.BlockSpec(memory_space=pltpu.HBM)
    dma = pltpu.SemaphoreType.DMA
    handed = pl.pallas_call(
        functools.partial(kernel, n),
        out_shape=(
            pltpu.VMEM((F, 2, HALF * H, 2 * C), f32),
            pltpu.VMEM((2, F, H, HALF, 256), bf16),
            pltpu.VMEM((2, F, H, HALF, 128), bf16),
            pltpu.VMEM((3 * C, 2 * C), bf16),
        ),
        in_specs=[hbm] * 7,
        out_specs=[vmem] * 4,
        scratch_shapes=[
            pltpu.VMEM((C,), f32), pltpu.VMEM((C,), f32), pltpu.VMEM((C,), f32),
            pltpu.VMEM((frames, block), bf16),
            pltpu.VMEM((frames + 16, block), f32),
            pltpu.VMEM((n, 8, block), bf16),
            pltpu.VMEM((n, 8, block), bf16),
            pltpu.VMEM((block // 128, n * 8, 128), f32),
            pltpu.VMEM((2, 3, (F + 4) * H, ROW), bf16),
            pltpu.VMEM((9, 3 * ZC, C), bf16),
            pltpu.VMEM((9 * 128, GROUP * C), bf16),
            pltpu.VMEM((4, 3, 3 * C, C), bf16),
            pltpu.VMEM((4, W + 2, H, C), bf16),
            pltpu.VMEM((W, F, H, C), bf16),
            pltpu.VMEM((4, HALF * H, 3 * 256), f32),
            pltpu.VMEM((4, HALF * H, 128), f32),
            pltpu.VMEM((2, F, H, HALF, 256), bf16), pltpu.VMEM((2, F, H, HALF, 128), bf16),
            dma((n,)), dma((n,)), dma((4,)), dma((4,)), dma(()), dma((9,)), dma(()), dma(()), dma((3,)),
        ],
        compiler_params=pltpu.CompilerParams(
            collective_id=0, has_side_effects=True, vmem_limit_bytes=44000000
        ),
        name="decoder_window",
    )(
        *(
            pltpu.with_memory_space_constraint(x, pltpu.HBM)
            for x in (
                latent, w_in.reshape(9, 3 * ZC, C), b_in, gain, w_mid.reshape(3, 3, 3 * C, C), b_mid,
                w_time.reshape(3 * C, 2 * C),
            )
        )
    )
    handed = [pltpu.with_memory_space_constraint(x, pltpu.VMEM) for x in handed]
    return pl.pallas_call(
        finish,
        out_shape=jax.ShapeDtypeStruct((2 * F, H, W, C), bf16),
        in_specs=[vmem] * 5,
        out_specs=hbm,
        scratch_shapes=[pltpu.VMEM((2, 2 * F, H, HALF, C), bf16), dma((2, 2 * F))],
        compiler_params=pltpu.CompilerParams(vmem_limit_bytes=44000000),
        name="finish",
    )(*handed, b_time)


def solution(mesh):
    n = mesh.shape["tm"]
    return jax.shard_map(
        functools.partial(per_device, n),
        mesh=mesh,
        in_specs=(P("groups", "tm"), P(), P(), P(), P(), P(), P(), P()),
        out_specs=P(("groups", "tm"), None, None, None),
        check_vma=False,
    )
```

```python
import functools

import jax
import jax.numpy as jnp
from jax import lax
from jax.experimental import pallas as pl
from jax.experimental.pallas import tpu as pltpu
from jax.sharding import PartitionSpec as P

ZC = 16
C = 384
H = 16
W = 32
F = 2
ROW = W * ZC
WIDE = ROW + 128
GROUP = 4
HALF = W // 2
PARTS = ((0, 256), (256, 128))
MESH = pl.DeviceIdType.MESH


def kernel(
    n, latent_ref, w_in_ref, b_in_ref, gain_ref, w_mid_ref, b_mid_ref, w_time_ref,
    part, halo_b, wtime,
    b_in, gain, b_mid, mine, padded, sent, got, spread, rolled, win, band, wmid, mixed, hid, product, turn, own_a, own_b, halo_a,
    lat_send, lat_recv, halo_send, halo_recv, win_sem, wmid_sem, wtime_sem, mine_sem, vec_sem,
):
    bf16, f32 = jnp.bfloat16, jnp.float32
    me = lax.axis_index("tm")
    block = latent_ref.shape[1]
    frames = latent_ref.shape[0]
    per_row = ROW // block

    mine_copy = pltpu.make_async_copy(latent_ref, mine, mine_sem)
    mine_copy.start()

    win_copy = pltpu.make_async_copy(w_in_ref, win, win_sem)
    vectors = ((b_in_ref, b_in), (gain_ref, gain), (b_mid_ref, b_mid))
    vec_copies = [
        pltpu.make_async_copy(src, dst, vec_sem.at[v]) for v, (src, dst) in enumerate(vectors)
    ]
    mid_copies = [
        [
            pltpu.make_async_copy(
                w_mid_ref.at[dt, di], wmid.at[(0, 1, 3)[dt], di], wmid_sem.at[di * 3 + dt]
            )
            for dt in range(3)
        ]
        for di in range(3)
    ]
    wtime_copy = pltpu.make_async_copy(w_time_ref, wtime, wtime_sem)

    def fetch():
        win_copy.start()
        for copy in vec_copies:
            copy.start()
        for copies in mid_copies:
            for copy in copies:
                copy.start()
        wtime_copy.start()

    barrier = pltpu.get_barrier_semaphore()

    def other(o):
        return lax.rem(me + o, n)

    def greet(o, carry):
        pl.semaphore_signal(barrier, inc=1, device_id={"tm": other(o)}, device_id_type=MESH)
        return carry

    lax.fori_loop(1, n, greet, 0, unroll=3)
    fetch()

    padded[pl.ds(0, 8), :] = jnp.zeros((8, block), f32)
    padded[pl.ds(frames, 16), :] = jnp.zeros((16, block), f32)
    mine_copy.wait()
    padded[pl.ds(4, frames), :] = mine[...].astype(f32)
    for d in range(n):
        sent[d] = padded[pl.ds(F * d, 8), :].astype(bf16)

    def combine(di):
        for copy in mid_copies[di]:
            copy.wait()

        def step(q, carry):
            here = (di, pl.ds(pl.multiple_of(q * 64, 64), 64))
            outer = wmid[0, *here].astype(f32) + wmid[3, *here].astype(f32)
            inner = wmid[1, *here].astype(f32)
            wmid[1, *here] = (outer + inner).astype(bf16)
            wmid[2, *here] = (outer - inner).astype(bf16)
            return carry

        lax.fori_loop(0, 3 * C // 64, step, 0)

    pl.semaphore_wait(barrier, n - 1)

    def lat_copy(d, j):
        return pltpu.make_async_remote_copy(
            src_ref=sent.at[d], dst_ref=got.at[j], send_sem=lat_send.at[d],
            recv_sem=lat_recv.at[j], device_id={"tm": d}, device_id_type=MESH,
        )

    def send(o, carry):
        lat_copy(other(o), me).start()
        return carry

    lax.fori_loop(1, n, send, 0, unroll=3)

    def clear(t, carry):
        band[pl.ds(t * 128, 128), :] = jnp.zeros((128, GROUP * C), bf16)
        return carry

    lax.fori_loop(0, 9, clear, 0)
    for m in range(4):
        mixed[m, 0] = jnp.zeros((H, C), bf16)
        mixed[m, W + 1] = jnp.zeros((H, C), bf16)
    got[me] = sent[me]
    win_copy.wait()
    for t in range(9):
        for c in range(GROUP):
            band[pl.ds(t * 128 + ZC * c, 3 * ZC), pl.ds(c * C, C)] = win[t]
    for copy in vec_copies:
        copy.wait()

    for di in range(0, 3):
        combine(di)

    def receive(o, carry):
        lat_copy(other(o), other(o)).wait_recv()
        return carry

    lax.fori_loop(1, n, receive, 0, unroll=3)

    flat = got[...].astype(f32).reshape(n * 8, block)
    for c in range(block // 128):
        spread[c] = flat[:, c * 128 : (c + 1) * 128]
    picked = []
    for s in range(F + 4):
        parts = [
            spread[c, pl.ds(b * 8 + s, H, stride=8 * per_row), :]
            for b in range(per_row)
            for c in range(block // 128)
        ]
        parts.append(jnp.zeros((H, 128), f32))
        picked.append(jnp.concatenate(parts, axis=1))
    lat = jnp.concatenate(picked, axis=0)
    total = (F + 4) * H
    row_of = lax.broadcasted_iota(jnp.int32, (total, ROW), 0) & (H - 1)
    for r in range(2):
        turned = pltpu.roll(lat, (ZC, WIDE - 3 * ZC)[r], 1)[:, :ROW]
        for di in range(3):
            if di == 0:
                moved = jnp.where(row_of == 0, 0.0, pltpu.roll(turned, 1, 0))
            elif di == 2:
                moved = jnp.where(row_of == H - 1, 0.0, pltpu.roll(turned, total - 1, 0))
            else:
                moved = turned
            rolled[r, di] = moved.astype(bf16)

    wide = (F + 2) * H
    keep = jnp.where(me > 0, 1.0, 0.0)

    def columns(r, carry):
        left = jnp.concatenate(
            [
                jnp.concatenate(
                    [
                        rolled[r, t % 3, pl.ds((t // 3) * H, wide), pl.ds(128 * b, 128)]
                        for b in range(4)
                    ],
                    axis=0,
                )
                for t in range(9)
            ],
            axis=1,
        )
        for pair in range(2):
            both = jnp.dot(
                left, band[:, pl.ds(pair * 2 * C, 2 * C)], preferred_element_type=f32
            )
            for c in range(2):
                h0 = (both[:, c * C : (c + 1) * C] + b_in[...][None, :]).astype(bf16)
                values = h0.astype(f32)
                scale = lax.rsqrt(jnp.mean(values * values, axis=-1, keepdims=True) + 1e-06)
                half = values * (0.5 * scale) * gain[...][None, :]
                act = half + half * jnp.tanh(half)
                for b in range(4):
                    w = 8 * b + 4 * r + 2 * pair + c
                    d0, d1, d2, d3 = (
                        act[b * wide + f * H : b * wide + (f + 1) * H] for f in range(4)
                    )
                    d0, d1 = d0 * keep, d1 * keep
                    mixed[0, w + 1] = (d0 - d2).astype(bf16)
                    mixed[1, w + 1] = (0.5 * (d1 + d2)).astype(bf16)
                    mixed[2, w + 1] = (0.5 * (d2 - d1)).astype(bf16)
                    mixed[3, w + 1] = (d1 - d3).astype(bf16)
                    for a in range(F):
                        hid[w, a] = h0[b * wide + (a + 2) * H : b * wide + (a + 3) * H]
        return carry

    for r in range(2):
        columns(r, 0)

    after = lax.rem(me + 1, n)

    own, halo = (own_a, own_b), (halo_a, halo_b)

    def halo_copy(h, p):
        return pltpu.make_async_remote_copy(
            src_ref=own[p].at[h], dst_ref=halo[p].at[h],
            send_sem=halo_send.at[h * 2 + p], recv_sem=halo_recv.at[h * 2 + p],
            device_id={"tm": after}, device_id_type=MESH,
        )

    rows = HALF * H

    def residual(h, carry):
        w0 = pl.multiple_of(h * HALF, HALF)
        for p, (c0, width) in enumerate(PARTS):
            for m in range(4):
                left = jnp.concatenate(
                    [mixed[m, pl.ds(w0 + dj, HALF)].reshape(rows, C) for dj in range(3)], axis=1
                )
                product[m, :, pl.ds(0, 3 * width)] = jnp.dot(
                    left,
                    jnp.concatenate(
                        [wmid[m, di, :, pl.ds(c0, width)] for di in range(3)], axis=1
                    ),
                    preferred_element_type=f32,
                )
            p0, p1, p2, p3 = (product[m, :, pl.ds(0, 3 * width)] for m in range(4))
            row = lax.broadcasted_iota(jnp.int32, (rows, width), 0) & (H - 1)
            for f, three in enumerate((p0 + p1 + p2, p1 - p2 - p3)):
                above = pltpu.roll(three[:, :width], 1, 0)
                below = pltpu.roll(three[:, 2 * width :], rows - 1, 0)
                acc = hid[pl.ds(w0, HALF), f, :, pl.ds(c0, width)].astype(f32).reshape(rows, width)
                acc = acc + b_mid[pl.ds(c0, width)][None, :] + three[:, width : 2 * width]
                acc = acc + jnp.where(row == 0, 0.0, above) + jnp.where(row == H - 1, 0.0, below)
                for c in range(width // 128):
                    turn[f * 2 + c] = acc[:, c * 128 : (c + 1) * 128]
                for i in range(H):
                    line = [
                        turn[f * 2 + c, pl.ds(i, HALF, stride=H), :] for c in range(width // 128)
                    ]
                    own[p][h, f, i] = jnp.concatenate(
                        line, axis=1
                    ).astype(bf16)

            @pl.when(me < n - 1)
            def _():
                halo_copy(h, p).start()

        return carry

    lax.fori_loop(0, 2, residual, 0)

    wtime_copy.wait()

    def both(pair, h, f):
        return jnp.concatenate(
            [ref[h, f].reshape(rows, width) for ref, (_, width) in zip(pair, PARTS)], axis=1
        )

    for h in range(2):
        mine0, mine1 = (both(own, h, f) for f in range(F))
        part[0, h] = jnp.dot(mine0, wtime[pl.ds(2 * C, C)], preferred_element_type=f32)
        part[1, h] = jnp.dot(
            jnp.concatenate([mine0, mine1], axis=1), wtime[pl.ds(C, 2 * C)],
            preferred_element_type=f32,
        )

    def sent_all(o, carry):
        lat_copy(other(o), me).wait_send()
        return carry

    lax.fori_loop(1, n, sent_all, 0)

    @pl.when(me > 0)
    def _():
        for h, p in ((0, 0), (0, 1), (1, 0), (1, 1)):
            halo_copy(h, p).wait_recv()
            if (h, p) != (1, 1):
                c0, width = PARTS[p]
                past0, past1 = (halo[p][h, f].reshape(rows, width) for f in range(F))
                part[0, h] += jnp.dot(
                    jnp.concatenate([past0, past1], axis=1),
                    jnp.concatenate([wtime[pl.ds(f * C + c0, width)] for f in range(F)], axis=0),
                    preferred_element_type=f32,
                )
                part[1, h] += jnp.dot(
                    past1, wtime[pl.ds(c0, width)], preferred_element_type=f32
                )

    @pl.when(me == 0)
    def _():
        halo_b[1] = jnp.zeros(halo_b.shape[1:], bf16)

    @pl.when(me < n - 1)
    def _():
        for h in range(2):
            for p in range(2):
                halo_copy(h, p).wait_send()


def finish(part, halo_b, wtime, b_time, out_ref, staged, out_sem):
    rows = HALF * H

    def out_copy(h, e):
        return pltpu.make_async_copy(
            staged.at[h, e], out_ref.at[e, :, pl.ds(h * HALF, HALF)], out_sem.at[h, e]
        )

    def put(h, f, up):
        up = (up + b_time[...][None, :]).astype(jnp.bfloat16)
        for s in range(2):
            staged[h, 2 * f + s] = up[:, s * C : (s + 1) * C].reshape(H, HALF, C)
            out_copy(h, 2 * f + s).start()

    for f in range(F):
        put(0, f, part[f, 0])
    c0, width = PARTS[1]
    past0, past1 = (halo_b[1, f].reshape(rows, width) for f in range(F))
    put(
        1, 0,
        part[0, 1]
        + jnp.dot(
            jnp.concatenate([past0, past1], axis=1),
            jnp.concatenate([wtime[pl.ds(f * C + c0, width)] for f in range(F)], axis=0),
            preferred_element_type=jnp.float32,
        ),
    )
    put(
        1, 1,
        part[1, 1]
        + jnp.dot(past1, wtime[pl.ds(c0, width)], preferred_element_type=jnp.float32),
    )
    for h in range(2):
        for e in range(2 * F):
            out_copy(h, e).wait()


def per_device(n, latent, w_in, b_in, gain, w_mid, b_mid, w_time, b_time):
    frames, block = latent.shape
    assert frames == F * n
    bf16, f32 = jnp.bfloat16, jnp.float32
    vmem = pl.BlockSpec(memory_space=pltpu.VMEM)
    hbm = pl.BlockSpec(memory_space=pltpu.HBM)
    dma = pltpu.SemaphoreType.DMA
    handed = pl.pallas_call(
        functools.partial(kernel, n),
        out_shape=(
            pltpu.VMEM((F, 2, HALF * H, 2 * C), f32),
            pltpu.VMEM((2, F, H, HALF, 128), bf16),
            pltpu.VMEM((3 * C, 2 * C), bf16),
        ),
        in_specs=[hbm] * 7,
        out_specs=[vmem] * 3,
        scratch_shapes=[
            pltpu.VMEM((C,), f32), pltpu.VMEM((C,), f32), pltpu.VMEM((C,), f32),
            pltpu.VMEM((frames, block), bf16),
            pltpu.VMEM((frames + 16, block), f32),
            pltpu.VMEM((n, 8, block), bf16),
            pltpu.VMEM((n, 8, block), bf16),
            pltpu.VMEM((block // 128, n * 8, 128), f32),
            pltpu.VMEM((2, 3, (F + 4) * H, ROW), bf16),
            pltpu.VMEM((9, 3 * ZC, C), bf16),
            pltpu.VMEM((9 * 128, GROUP * C), bf16),
            pltpu.VMEM((4, 3, 3 * C, C), bf16),
            pltpu.VMEM((4, W + 2, H, C), bf16),
            pltpu.VMEM((W, F, H, C), bf16),
            pltpu.VMEM((4, HALF * H, 3 * 256), f32),
            pltpu.VMEM((4, HALF * H, 128), f32),
            pltpu.VMEM((2, F, H, HALF, 256), bf16), pltpu.VMEM((2, F, H, HALF, 128), bf16),
            pltpu.VMEM((2, F, H, HALF, 256), bf16),
            dma((n,)), dma((n,)), dma((4,)), dma((4,)), dma(()), dma((9,)), dma(()), dma(()), dma((3,)),
        ],
        compiler_params=pltpu.CompilerParams(
            collective_id=0, has_side_effects=True, vmem_limit_bytes=44000000
        ),
        name="decoder_window",
    )(
        *(
            pltpu.with_memory_space_constraint(x, pltpu.HBM)
            for x in (
                latent, w_in.reshape(9, 3 * ZC, C), b_in, gain, w_mid.reshape(3, 3, 3 * C, C), b_mid,
                w_time.reshape(3 * C, 2 * C),
            )
        )
    )
    handed = [pltpu.with_memory_space_constraint(x, pltpu.VMEM) for x in handed]
    return pl.pallas_call(
        finish,
        out_shape=jax.ShapeDtypeStruct((2 * F, H, W, C), bf16),
        in_specs=[vmem] * 4,
        out_specs=hbm,
        scratch_shapes=[pltpu.VMEM((2, 2 * F, H, HALF, C), bf16), dma((2, 2 * F))],
        compiler_params=pltpu.CompilerParams(vmem_limit_bytes=44000000),
        name="finish",
    )(*handed, b_time)


def solution(mesh):
    n = mesh.shape["tm"]
    return jax.shard_map(
        functools.partial(per_device, n),
        mesh=mesh,
        in_specs=(P("groups", "tm"), P(), P(), P(), P(), P(), P(), P()),
        out_specs=P(("groups", "tm"), None, None, None),
        check_vma=False,
    )
```

```python
import functools

import jax
import jax.numpy as jnp
from jax import lax
from jax.experimental import pallas as pl
from jax.experimental.pallas import tpu as pltpu
from jax.sharding import PartitionSpec as P

ZC = 16
C = 384
H = 16
W = 32
F = 2
ROW = W * ZC
WIDE = ROW + 128
GROUP = 4
HALF = W // 2
PARTS = ((0, 256), (256, 128))
MESH = pl.DeviceIdType.MESH


def kernel(
    n, latent_ref, w_in_ref, b_in_ref, gain_ref, w_mid_ref, b_mid_ref, w_time_ref, b_time_ref,
    part, halo_b, wtime, ready,
    b_in, gain, b_mid, b_time, mine, padded, sent, got, spread, rolled, win, band, wmid, mixed, hid, product, turn, own_a, own_b, halo_a,
    lat_send, lat_recv, halo_send, halo_recv, win_sem, wmid_sem, wtime_sem, mine_sem, vec_sem,
):
    bf16, f32 = jnp.bfloat16, jnp.float32
    me = lax.axis_index("tm")
    block = latent_ref.shape[1]
    frames = latent_ref.shape[0]
    per_row = ROW // block
    packed = sent.shape[2]

    mine_copy = pltpu.make_async_copy(latent_ref, mine, mine_sem)
    mine_copy.start()

    win_copy = pltpu.make_async_copy(w_in_ref, win, win_sem)
    vectors = ((b_in_ref, b_in), (gain_ref, gain), (b_mid_ref, b_mid), (b_time_ref, b_time))
    vec_copies = [
        pltpu.make_async_copy(src, dst, vec_sem.at[v]) for v, (src, dst) in enumerate(vectors)
    ]
    mid_copies = [
        [
            pltpu.make_async_copy(
                w_mid_ref.at[dt, di], wmid.at[(0, 1, 3)[dt], di], wmid_sem.at[di * 3 + dt]
            )
            for dt in range(3)
        ]
        for di in range(3)
    ]
    wtime_copy = pltpu.make_async_copy(w_time_ref, wtime, wtime_sem)

    def fetch():
        win_copy.start()
        for copy in vec_copies:
            copy.start()
        for copies in mid_copies:
            for copy in copies:
                copy.start()
        wtime_copy.start()

    barrier = pltpu.get_barrier_semaphore()

    def other(o):
        return lax.rem(me + o, n)

    def greet(o, carry):
        pl.semaphore_signal(barrier, inc=1, device_id={"tm": other(o)}, device_id_type=MESH)
        return carry

    for o in range(1, n):
        greet(o, 0)
    fetch()

    padded[pl.ds(0, 8), :] = jnp.zeros((8, block), f32)
    padded[pl.ds(frames, 16), :] = jnp.zeros((16, block), f32)
    mine_copy.wait()
    padded[pl.ds(4, frames), :] = mine[...].astype(f32)
    for d in range(n):
        window = padded[pl.ds(F * d, 8), :]
        if packed < block:
            last = window[:, packed:]
            row = lax.broadcasted_iota(jnp.int32, (8, 128), 0)
            window = jnp.concatenate(
                [
                    jnp.where(
                        row < F + 4, window[:, c * 128 : (c + 1) * 128],
                        pltpu.roll(last, 6 - 2 * c, 0),
                    )
                    for c in range(3)
                ],
                axis=1,
            )
        sent[d] = window.astype(bf16)

    def combine(di):
        for copy in mid_copies[di]:
            copy.wait()

        def step(q, carry):
            here = (di, pl.ds(pl.multiple_of(q * 64, 64), 64))
            outer = wmid[0, *here].astype(f32) + wmid[3, *here].astype(f32)
            inner = wmid[1, *here].astype(f32)
            wmid[1, *here] = (outer + inner).astype(bf16)
            wmid[2, *here] = (outer - inner).astype(bf16)
            return carry

        lax.fori_loop(0, 3 * C // 64, step, 0)

    pl.semaphore_wait(barrier, n - 1)

    def lat_copy(d, j):
        return pltpu.make_async_remote_copy(
            src_ref=sent.at[d], dst_ref=got.at[j], send_sem=lat_send.at[d],
            recv_sem=lat_recv.at[j], device_id={"tm": d}, device_id_type=MESH,
        )

    def send(o, carry):
        lat_copy(other(o), me).start()
        return carry

    for o in range(1, n):
        send(o, 0)

    def clear(t, carry):
        band[pl.ds(t * 128, 128), :] = jnp.zeros((128, GROUP * C), bf16)
        return carry

    lax.fori_loop(0, 9, clear, 0)
    for m in range(4):
        mixed[m, 0] = jnp.zeros((H, C), bf16)
        mixed[m, W + 1] = jnp.zeros((H, C), bf16)
    got[me] = sent[me]
    win_copy.wait()
    for t in range(9):
        for c in range(GROUP):
            band[pl.ds(t * 128 + ZC * c, 3 * ZC), pl.ds(c * C, C)] = win[t]
    for copy in vec_copies:
        copy.wait()

    for di in range(0, 3):
        combine(di)

    def receive(o, carry):
        lat_copy(other(o), other(o)).wait_recv()
        return carry

    for o in range(1, n):
        receive(o, 0)

    flat = got[...].astype(f32).reshape(n * 8, packed)
    for c in range(packed // 128):
        spread[c] = flat[:, c * 128 : (c + 1) * 128]
    picked = []
    for s in range(F + 4):
        parts = [
            spread[c, pl.ds(b * 8 + s, H, stride=8 * per_row), :]
            if c < packed // 128
            else spread[s // 2, pl.ds(b * 8 + 6 + s % 2, H, stride=8 * per_row), :]
            for b in range(per_row)
            for c in range(block // 128)
        ]
        parts.append(jnp.zeros((H, 128), f32))
        picked.append(jnp.concatenate(parts, axis=1))
    lat = jnp.concatenate(picked, axis=0)
    total = (F + 4) * H
    row_of = lax.broadcasted_iota(jnp.int32, (total, ROW), 0) & (H - 1)
    for r in range(2):
        turned = pltpu.roll(lat, (ZC, WIDE - 3 * ZC)[r], 1)[:, :ROW]
        for di in range(3):
            if di == 0:
                moved = jnp.where(row_of == 0, 0.0, pltpu.roll(turned, 1, 0))
            elif di == 2:
                moved = jnp.where(row_of == H - 1, 0.0, pltpu.roll(turned, total - 1, 0))
            else:
                moved = turned
            rolled[r, di] = moved.astype(bf16)

    wide = (F + 2) * H
    keep = jnp.where(me > 0, 1.0, 0.0)

    def columns(r, carry):
        left = jnp.concatenate(
            [
                jnp.concatenate(
                    [
                        rolled[r, t % 3, pl.ds((t // 3) * H, wide), pl.ds(128 * b, 128)]
                        for b in range(4)
                    ],
                    axis=0,
                )
                for t in range(9)
            ],
            axis=1,
        )
        for pair in range(2):
            both = jnp.dot(
                left, band[:, pl.ds(pair * 2 * C, 2 * C)], preferred_element_type=f32
            )
            for c in range(2):
                h0 = (both[:, c * C : (c + 1) * C] + b_in[...][None, :]).astype(bf16)
                values = h0.astype(f32)
                scale = lax.rsqrt(jnp.mean(values * values, axis=-1, keepdims=True) + 1e-06)
                half = values * (0.5 * scale) * gain[...][None, :]
                act = half + half * jnp.tanh(half)
                for b in range(4):
                    w = 8 * b + 4 * r + 2 * pair + c
                    d0, d1, d2, d3 = (
                        act[b * wide + f * H : b * wide + (f + 1) * H] for f in range(4)
                    )
                    d0, d1 = d0 * keep, d1 * keep
                    mixed[0, w + 1] = (d0 - d2).astype(bf16)
                    mixed[1, w + 1] = (0.5 * (d1 + d2)).astype(bf16)
                    mixed[2, w + 1] = (0.5 * (d2 - d1)).astype(bf16)
                    mixed[3, w + 1] = (d1 - d3).astype(bf16)
                    for a in range(F):
                        hid[w, a] = h0[b * wide + (a + 2) * H : b * wide + (a + 3) * H]
        return carry

    for r in range(2):
        columns(r, 0)

    after = lax.rem(me + 1, n)

    own, halo = (own_a, own_b), (halo_a, halo_b)

    def halo_copy(h, p):
        return pltpu.make_async_remote_copy(
            src_ref=own[p].at[h], dst_ref=halo[p].at[h],
            send_sem=halo_send.at[h * 2 + p], recv_sem=halo_recv.at[h * 2 + p],
            device_id={"tm": after}, device_id_type=MESH,
        )

    rows = HALF * H

    def residual(h, carry):
        w0 = pl.multiple_of(h * HALF, HALF)
        for p, (c0, width) in enumerate(PARTS):
            for m in range(4):
                left = jnp.concatenate(
                    [mixed[m, pl.ds(w0 + dj, HALF)].reshape(rows, C) for dj in range(3)], axis=1
                )
                product[m, :, pl.ds(0, 3 * width)] = jnp.dot(
                    left,
                    jnp.concatenate(
                        [wmid[m, di, :, pl.ds(c0, width)] for di in range(3)], axis=1
                    ),
                    preferred_element_type=f32,
                )
            p0, p1, p2, p3 = (product[m, :, pl.ds(0, 3 * width)] for m in range(4))
            row = lax.broadcasted_iota(jnp.int32, (rows, width), 0) & (H - 1)
            for f, three in enumerate((p0 + p1 + p2, p1 - p2 - p3)):
                above = pltpu.roll(three[:, :width], 1, 0)
                below = pltpu.roll(three[:, 2 * width :], rows - 1, 0)
                acc = hid[pl.ds(w0, HALF), f, :, pl.ds(c0, width)].astype(f32).reshape(rows, width)
                acc = acc + b_mid[pl.ds(c0, width)][None, :] + three[:, width : 2 * width]
                acc = acc + jnp.where(row == 0, 0.0, above) + jnp.where(row == H - 1, 0.0, below)
                for c in range(width // 128):
                    turn[f * 2 + c] = acc[:, c * 128 : (c + 1) * 128]
                for i in range(H):
                    line = [
                        turn[f * 2 + c, pl.ds(i, HALF, stride=H), :] for c in range(width // 128)
                    ]
                    own[p][h, f, i] = jnp.concatenate(
                        line, axis=1
                    ).astype(bf16)

            @pl.when(me < n - 1)
            def _():
                halo_copy(h, p).start()

        return carry

    lax.fori_loop(0, 2, residual, 0)

    wtime_copy.wait()

    def both(pair, h, f):
        return jnp.concatenate(
            [ref[h, f].reshape(rows, width) for ref, (_, width) in zip(pair, PARTS)], axis=1
        )

    for h in range(2):
        mine0, mine1 = (both(own, h, f) for f in range(F))
        part[0, h] = jnp.dot(mine0, wtime[pl.ds(2 * C, C)], preferred_element_type=f32)
        part[1, h] = jnp.dot(
            jnp.concatenate([mine0, mine1], axis=1), wtime[pl.ds(C, 2 * C)],
            preferred_element_type=f32,
        )

    def sent_all(o, carry):
        lat_copy(other(o), me).wait_send()
        return carry

    lax.fori_loop(1, n, sent_all, 0)

    def gather(h, p):
        halo_copy(h, p).wait_recv()
        if (h, p) != (1, 1):
            c0, width = PARTS[p]
            past0, past1 = (halo[p][h, f].reshape(rows, width) for f in range(F))
            part[0, h] += jnp.dot(
                jnp.concatenate([past0, past1], axis=1),
                jnp.concatenate([wtime[pl.ds(f * C + c0, width)] for f in range(F)], axis=0),
                preferred_element_type=f32,
            )
            part[1, h] += jnp.dot(past1, wtime[pl.ds(c0, width)], preferred_element_type=f32)

    @pl.when(me > 0)
    def _():
        gather(0, 0)
        gather(0, 1)

    for f in range(F):
        up = (part[f, 0] + b_time[...][None, :]).astype(bf16)
        for s in range(2):
            ready[2 * f + s] = up[:, s * C : (s + 1) * C].reshape(H, HALF, C)

    @pl.when(me > 0)
    def _():
        gather(1, 0)
        gather(1, 1)

    @pl.when(me == 0)
    def _():
        halo_b[1] = jnp.zeros(halo_b.shape[1:], bf16)

    @pl.when(me < n - 1)
    def _():
        for h in range(2):
            for p in range(2):
                halo_copy(h, p).wait_send()


def finish(part, halo_b, wtime, ready, b_time, out_ref, staged, out_sem):
    rows = HALF * H

    def out_copy(h, e):
        return pltpu.make_async_copy(
            (ready, staged)[h].at[e], out_ref.at[e, :, pl.ds(h * HALF, HALF)], out_sem.at[h, e]
        )

    def put(h, f, up):
        up = (up + b_time[...][None, :]).astype(jnp.bfloat16)
        for s in range(2):
            staged[2 * f + s] = up[:, s * C : (s + 1) * C].reshape(H, HALF, C)
            out_copy(h, 2 * f + s).start()

    for e in range(2 * F):
        out_copy(0, e).start()
    c0, width = PARTS[1]
    past0, past1 = (halo_b[1, f].reshape(rows, width) for f in range(F))
    put(
        1, 0,
        part[0, 1]
        + jnp.dot(
            jnp.concatenate([past0, past1], axis=1),
            jnp.concatenate([wtime[pl.ds(f * C + c0, width)] for f in range(F)], axis=0),
            preferred_element_type=jnp.float32,
        ),
    )
    put(
        1, 1,
        part[1, 1]
        + jnp.dot(past1, wtime[pl.ds(c0, width)], preferred_element_type=jnp.float32),
    )
    for h in range(2):
        for e in range(2 * F):
            out_copy(h, e).wait()


def per_device(n, latent, w_in, b_in, gain, w_mid, b_mid, w_time, b_time):
    frames, block = latent.shape
    assert frames == F * n
    bf16, f32 = jnp.bfloat16, jnp.float32
    packed = block * 3 // 4 if block == 512 else block
    vmem = pl.BlockSpec(memory_space=pltpu.VMEM)
    hbm = pl.BlockSpec(memory_space=pltpu.HBM)
    dma = pltpu.SemaphoreType.DMA
    handed = pl.pallas_call(
        functools.partial(kernel, n),
        out_shape=(
            pltpu.VMEM((F, 2, HALF * H, 2 * C), f32),
            pltpu.VMEM((2, F, H, HALF, 128), bf16),
            pltpu.VMEM((3 * C, 2 * C), bf16),
            pltpu.VMEM((2 * F, H, HALF, C), bf16),
        ),
        in_specs=[hbm] * 8,
        out_specs=[vmem] * 4,
        scratch_shapes=[
            pltpu.VMEM((C,), f32), pltpu.VMEM((C,), f32), pltpu.VMEM((C,), f32),
            pltpu.VMEM((2 * C,), f32),
            pltpu.VMEM((frames, block), bf16),
            pltpu.VMEM((frames + 16, block), f32),
            pltpu.VMEM((n, 8, packed), bf16),
            pltpu.VMEM((n, 8, packed), bf16),
            pltpu.VMEM((block // 128, n * 8, 128), f32),
            pltpu.VMEM((2, 3, (F + 4) * H, ROW), bf16),
            pltpu.VMEM((9, 3 * ZC, C), bf16),
            pltpu.VMEM((9 * 128, GROUP * C), bf16),
            pltpu.VMEM((4, 3, 3 * C, C), bf16),
            pltpu.VMEM((4, W + 2, H, C), bf16),
            pltpu.VMEM((W, F, H, C), bf16),
            pltpu.VMEM((4, HALF * H, 3 * 256), f32),
            pltpu.VMEM((4, HALF * H, 128), f32),
            pltpu.VMEM((2, F, H, HALF, 256), bf16), pltpu.VMEM((2, F, H, HALF, 128), bf16),
            pltpu.VMEM((2, F, H, HALF, 256), bf16),
            dma((n,)), dma((n,)), dma((4,)), dma((4,)), dma(()), dma((9,)), dma(()), dma(()), dma((4,)),
        ],
        compiler_params=pltpu.CompilerParams(
            collective_id=0, has_side_effects=True, vmem_limit_bytes=44000000
        ),
        name="decoder_window",
    )(
        *(
            pltpu.with_memory_space_constraint(x, pltpu.HBM)
            for x in (
                latent, w_in.reshape(9, 3 * ZC, C), b_in, gain, w_mid.reshape(3, 3, 3 * C, C), b_mid,
                w_time.reshape(3 * C, 2 * C), b_time,
            )
        )
    )
    handed = [pltpu.with_memory_space_constraint(x, pltpu.VMEM) for x in handed]
    return pl.pallas_call(
        finish,
        out_shape=jax.ShapeDtypeStruct((2 * F, H, W, C), bf16),
        in_specs=[vmem] * 5,
        out_specs=hbm,
        scratch_shapes=[pltpu.VMEM((2 * F, H, HALF, C), bf16), dma((2, 2 * F))],
        compiler_params=pltpu.CompilerParams(vmem_limit_bytes=44000000),
        name="finish",
    )(*handed, b_time)


def solution(mesh):
    n = mesh.shape["tm"]
    return jax.shard_map(
        functools.partial(per_device, n),
        mesh=mesh,
        in_specs=(P("groups", "tm"), P(), P(), P(), P(), P(), P(), P()),
        out_specs=P(("groups", "tm"), None, None, None),
        check_vma=False,
    )
```

```python
import functools

import jax
import jax.numpy as jnp
from jax import lax
from jax.experimental import pallas as pl
from jax.experimental.pallas import tpu as pltpu
from jax.sharding import PartitionSpec as P

ZC = 16
C = 384
H = 16
W = 32
F = 2
ROW = W * ZC
WIDE = ROW + 128
GROUP = 4
HALF = W // 2
PARTS = ((0, 256), (256, 128))
MESH = pl.DeviceIdType.MESH


def kernel(
    n, latent_ref, w_in_ref, b_in_ref, gain_ref, w_mid_ref, b_mid_ref, w_time_ref, b_time_ref,
    part, halo_b, wtime, ready,
    b_in, gain, b_mid, b_time, mine, padded, sent, got, spread, rolled, win, band, wmid, mixed, hid, product, turn, own_a, own_b, halo_a,
    lat_send, lat_recv, halo_send, halo_recv, win_sem, wmid_sem, wtime_sem, mine_sem, vec_sem,
):
    bf16, f32 = jnp.bfloat16, jnp.float32
    me = lax.axis_index("tm")
    block = latent_ref.shape[1]
    frames = latent_ref.shape[0]
    per_row = ROW // block
    packed = sent.shape[2]

    mine_copy = pltpu.make_async_copy(latent_ref, mine, mine_sem)
    mine_copy.start()

    win_copy = pltpu.make_async_copy(w_in_ref, win, win_sem)
    vectors = ((b_in_ref, b_in), (gain_ref, gain), (b_mid_ref, b_mid), (b_time_ref, b_time))
    vec_copies = [
        pltpu.make_async_copy(src, dst, vec_sem.at[v]) for v, (src, dst) in enumerate(vectors)
    ]
    mid_copies = [
        [
            pltpu.make_async_copy(
                w_mid_ref.at[dt, di], wmid.at[(0, 1, 3)[dt], di], wmid_sem.at[di * 3 + dt]
            )
            for dt in range(3)
        ]
        for di in range(3)
    ]
    wtime_copy = pltpu.make_async_copy(w_time_ref, wtime, wtime_sem)

    def fetch():
        win_copy.start()
        for copy in vec_copies:
            copy.start()
        for copies in mid_copies:
            for copy in copies:
                copy.start()
        wtime_copy.start()

    barrier = pltpu.get_barrier_semaphore()

    def other(o):
        return lax.rem(me + o, n)

    quad = me - lax.rem(me, 4)
    first = [(c, k) for c in (3, 1, 2, 0)[:2] for k in range(1, n // 4)]
    last = [(c, k) for c in (3, 1, 2, 0)[2:] for k in range(1, n // 4)]
    targets = [lax.rem(quad + 4 * k + c, n) for c, k in first]
    targets += [quad + lax.rem(me + j, 4) for j in range(1, 4)]
    targets += [lax.rem(quad + 4 * k + c, n) for c, k in last]

    def greet(o, carry):
        pl.semaphore_signal(barrier, inc=1, device_id={"tm": other(o)}, device_id_type=MESH)
        return carry

    for o in range(1, n):
        greet(o, 0)
    fetch()

    padded[pl.ds(0, 8), :] = jnp.zeros((8, block), f32)
    padded[pl.ds(frames, 16), :] = jnp.zeros((16, block), f32)
    mine_copy.wait()
    padded[pl.ds(4, frames), :] = mine[...].astype(f32)
    for d in range(n):
        window = padded[pl.ds(F * d, 8), :]
        if packed < block:
            last = window[:, packed:]
            row = lax.broadcasted_iota(jnp.int32, (8, 128), 0)
            window = jnp.concatenate(
                [
                    jnp.where(
                        row < F + 4, window[:, c * 128 : (c + 1) * 128],
                        pltpu.roll(last, 6 - 2 * c, 0),
                    )
                    for c in range(3)
                ],
                axis=1,
            )
        sent[d] = window.astype(bf16)

    def combine(di):
        for copy in mid_copies[di]:
            copy.wait()

        def step(q, carry):
            here = (di, pl.ds(pl.multiple_of(q * 64, 64), 64))
            outer = wmid[0, *here].astype(f32) + wmid[3, *here].astype(f32)
            inner = wmid[1, *here].astype(f32)
            wmid[1, *here] = (outer + inner).astype(bf16)
            wmid[2, *here] = (outer - inner).astype(bf16)
            return carry

        lax.fori_loop(0, 3 * C // 64, step, 0)

    pl.semaphore_wait(barrier, n - 1)

    def lat_copy(d, j):
        return pltpu.make_async_remote_copy(
            src_ref=sent.at[d], dst_ref=got.at[j], send_sem=lat_send.at[d],
            recv_sem=lat_recv.at[j], device_id={"tm": d}, device_id_type=MESH,
        )

    for d in targets:
        lat_copy(d, me).start()

    def clear(t, carry):
        band[pl.ds(t * 128, 128), :] = jnp.zeros((128, GROUP * C), bf16)
        return carry

    lax.fori_loop(0, 9, clear, 0)
    for m in range(4):
        mixed[m, 0] = jnp.zeros((H, C), bf16)
        mixed[m, W + 1] = jnp.zeros((H, C), bf16)
    got[me] = sent[me]
    win_copy.wait()
    for t in range(9):
        for c in range(GROUP):
            band[pl.ds(t * 128 + ZC * c, 3 * ZC), pl.ds(c * C, C)] = win[t]
    for copy in vec_copies:
        copy.wait()

    for di in range(0, 3):
        combine(di)

    def receive(o, carry):
        lat_copy(other(o), other(o)).wait_recv()
        return carry

    for o in range(1, n):
        receive(o, 0)

    flat = got[...].astype(f32).reshape(n * 8, packed)
    for c in range(packed // 128):
        spread[c] = flat[:, c * 128 : (c + 1) * 128]
    picked = []
    for s in range(F + 4):
        parts = [
            spread[c, pl.ds(b * 8 + s, H, stride=8 * per_row), :]
            if c < packed // 128
            else spread[s // 2, pl.ds(b * 8 + 6 + s % 2, H, stride=8 * per_row), :]
            for b in range(per_row)
            for c in range(block // 128)
        ]
        parts.append(jnp.zeros((H, 128), f32))
        picked.append(jnp.concatenate(parts, axis=1))
    lat = jnp.concatenate(picked, axis=0)
    total = (F + 4) * H
    row_of = lax.broadcasted_iota(jnp.int32, (total, ROW), 0) & (H - 1)
    for r in range(2):
        turned = pltpu.roll(lat, (ZC, WIDE - 3 * ZC)[r], 1)[:, :ROW]
        for di in range(3):
            if di == 0:
                moved = jnp.where(row_of == 0, 0.0, pltpu.roll(turned, 1, 0))
            elif di == 2:
                moved = jnp.where(row_of == H - 1, 0.0, pltpu.roll(turned, total - 1, 0))
            else:
                moved = turned
            rolled[r, di] = moved.astype(bf16)

    wide = (F + 2) * H
    keep = jnp.where(me > 0, 1.0, 0.0)

    def columns(r, carry):
        left = jnp.concatenate(
            [
                jnp.concatenate(
                    [
                        rolled[r, t % 3, pl.ds((t // 3) * H, wide), pl.ds(128 * b, 128)]
                        for b in range(4)
                    ],
                    axis=0,
                )
                for t in range(9)
            ],
            axis=1,
        )
        for pair in range(2):
            both = jnp.dot(
                left, band[:, pl.ds(pair * 2 * C, 2 * C)], preferred_element_type=f32
            )
            for c in range(2):
                h0 = (both[:, c * C : (c + 1) * C] + b_in[...][None, :]).astype(bf16)
                values = h0.astype(f32)
                scale = lax.rsqrt(jnp.mean(values * values, axis=-1, keepdims=True) + 1e-06)
                half = values * (0.5 * scale) * gain[...][None, :]
                act = half + half * jnp.tanh(half)
                for b in range(4):
                    w = 8 * b + 4 * r + 2 * pair + c
                    d0, d1, d2, d3 = (
                        act[b * wide + f * H : b * wide + (f + 1) * H] for f in range(4)
                    )
                    d0, d1 = d0 * keep, d1 * keep
                    mixed[0, w + 1] = (d0 - d2).astype(bf16)
                    mixed[1, w + 1] = (0.5 * (d1 + d2)).astype(bf16)
                    mixed[2, w + 1] = (0.5 * (d2 - d1)).astype(bf16)
                    mixed[3, w + 1] = (d1 - d3).astype(bf16)
                    for a in range(F):
                        hid[w, a] = h0[b * wide + (a + 2) * H : b * wide + (a + 3) * H]
        return carry

    for r in range(2):
        columns(r, 0)

    after = lax.rem(me + 1, n)

    own, halo = (own_a, own_b), (halo_a, halo_b)

    def halo_copy(h, p):
        return pltpu.make_async_remote_copy(
            src_ref=own[p].at[h], dst_ref=halo[p].at[h],
            send_sem=halo_send.at[h * 2 + p], recv_sem=halo_recv.at[h * 2 + p],
            device_id={"tm": after}, device_id_type=MESH,
        )

    rows = HALF * H

    def residual(h, carry):
        w0 = pl.multiple_of(h * HALF, HALF)
        for p, (c0, width) in enumerate(PARTS):
            for m in range(4):
                left = jnp.concatenate(
                    [mixed[m, pl.ds(w0 + dj, HALF)].reshape(rows, C) for dj in range(3)], axis=1
                )
                product[m, :, pl.ds(0, 3 * width)] = jnp.dot(
                    left,
                    jnp.concatenate(
                        [wmid[m, di, :, pl.ds(c0, width)] for di in range(3)], axis=1
                    ),
                    preferred_element_type=f32,
                )
            p0, p1, p2, p3 = (product[m, :, pl.ds(0, 3 * width)] for m in range(4))
            row = lax.broadcasted_iota(jnp.int32, (rows, width), 0) & (H - 1)
            for f, three in enumerate((p0 + p1 + p2, p1 - p2 - p3)):
                above = pltpu.roll(three[:, :width], 1, 0)
                below = pltpu.roll(three[:, 2 * width :], rows - 1, 0)
                acc = hid[pl.ds(w0, HALF), f, :, pl.ds(c0, width)].astype(f32).reshape(rows, width)
                acc = acc + b_mid[pl.ds(c0, width)][None, :] + three[:, width : 2 * width]
                acc = acc + jnp.where(row == 0, 0.0, above) + jnp.where(row == H - 1, 0.0, below)
                for c in range(width // 128):
                    turn[f * 2 + c] = acc[:, c * 128 : (c + 1) * 128]
                for i in range(H):
                    line = [
                        turn[f * 2 + c, pl.ds(i, HALF, stride=H), :] for c in range(width // 128)
                    ]
                    own[p][h, f, i] = jnp.concatenate(
                        line, axis=1
                    ).astype(bf16)

            @pl.when(me < n - 1)
            def _():
                halo_copy(h, p).start()

        return carry

    lax.fori_loop(0, 2, residual, 0)

    wtime_copy.wait()

    def both(pair, h, f):
        return jnp.concatenate(
            [ref[h, f].reshape(rows, width) for ref, (_, width) in zip(pair, PARTS)], axis=1
        )

    for h in range(2):
        mine0, mine1 = (both(own, h, f) for f in range(F))
        part[0, h] = jnp.dot(mine0, wtime[pl.ds(2 * C, C)], preferred_element_type=f32)
        part[1, h] = jnp.dot(
            jnp.concatenate([mine0, mine1], axis=1), wtime[pl.ds(C, 2 * C)],
            preferred_element_type=f32,
        )

    def sent_all(o, carry):
        lat_copy(other(o), me).wait_send()
        return carry

    lax.fori_loop(1, n, sent_all, 0)

    def gather(h, p):
        halo_copy(h, p).wait_recv()
        if (h, p) != (1, 1):
            c0, width = PARTS[p]
            past0, past1 = (halo[p][h, f].reshape(rows, width) for f in range(F))
            part[0, h] += jnp.dot(
                jnp.concatenate([past0, past1], axis=1),
                jnp.concatenate([wtime[pl.ds(f * C + c0, width)] for f in range(F)], axis=0),
                preferred_element_type=f32,
            )
            part[1, h] += jnp.dot(past1, wtime[pl.ds(c0, width)], preferred_element_type=f32)

    @pl.when(me > 0)
    def _():
        gather(0, 0)
        gather(0, 1)

    for f in range(F):
        up = (part[f, 0] + b_time[...][None, :]).astype(bf16)
        for s in range(2):
            ready[2 * f + s] = up[:, s * C : (s + 1) * C].reshape(H, HALF, C)

    @pl.when(me > 0)
    def _():
        gather(1, 0)
        gather(1, 1)

    @pl.when(me == 0)
    def _():
        halo_b[1] = jnp.zeros(halo_b.shape[1:], bf16)

    @pl.when(me < n - 1)
    def _():
        for h in range(2):
            for p in range(2):
                halo_copy(h, p).wait_send()


def finish(part, halo_b, wtime, ready, b_time, out_ref, staged, out_sem):
    rows = HALF * H

    def out_copy(h, e):
        return pltpu.make_async_copy(
            (ready, staged)[h].at[e], out_ref.at[e, :, pl.ds(h * HALF, HALF)], out_sem.at[h, e]
        )

    def put(h, f, up):
        up = (up + b_time[...][None, :]).astype(jnp.bfloat16)
        for s in range(2):
            staged[2 * f + s] = up[:, s * C : (s + 1) * C].reshape(H, HALF, C)
            out_copy(h, 2 * f + s).start()

    for e in range(2 * F):
        out_copy(0, e).start()
    c0, width = PARTS[1]
    past0, past1 = (halo_b[1, f].reshape(rows, width) for f in range(F))
    put(
        1, 0,
        part[0, 1]
        + jnp.dot(
            jnp.concatenate([past0, past1], axis=1),
            jnp.concatenate([wtime[pl.ds(f * C + c0, width)] for f in range(F)], axis=0),
            preferred_element_type=jnp.float32,
        ),
    )
    put(
        1, 1,
        part[1, 1]
        + jnp.dot(past1, wtime[pl.ds(c0, width)], preferred_element_type=jnp.float32),
    )
    for h in range(2):
        for e in range(2 * F):
            out_copy(h, e).wait()


def per_device(n, latent, w_in, b_in, gain, w_mid, b_mid, w_time, b_time):
    frames, block = latent.shape
    assert frames == F * n
    bf16, f32 = jnp.bfloat16, jnp.float32
    packed = block * 3 // 4 if block == 512 else block
    vmem = pl.BlockSpec(memory_space=pltpu.VMEM)
    hbm = pl.BlockSpec(memory_space=pltpu.HBM)
    dma = pltpu.SemaphoreType.DMA
    handed = pl.pallas_call(
        functools.partial(kernel, n),
        out_shape=(
            pltpu.VMEM((F, 2, HALF * H, 2 * C), f32),
            pltpu.VMEM((2, F, H, HALF, 128), bf16),
            pltpu.VMEM((3 * C, 2 * C), bf16),
            pltpu.VMEM((2 * F, H, HALF, C), bf16),
        ),
        in_specs=[hbm] * 8,
        out_specs=[vmem] * 4,
        scratch_shapes=[
            pltpu.VMEM((C,), f32), pltpu.VMEM((C,), f32), pltpu.VMEM((C,), f32),
            pltpu.VMEM((2 * C,), f32),
            pltpu.VMEM((frames, block), bf16),
            pltpu.VMEM((frames + 16, block), f32),
            pltpu.VMEM((n, 8, packed), bf16),
            pltpu.VMEM((n, 8, packed), bf16),
            pltpu.VMEM((block // 128, n * 8, 128), f32),
            pltpu.VMEM((2, 3, (F + 4) * H, ROW), bf16),
            pltpu.VMEM((9, 3 * ZC, C), bf16),
            pltpu.VMEM((9 * 128, GROUP * C), bf16),
            pltpu.VMEM((4, 3, 3 * C, C), bf16),
            pltpu.VMEM((4, W + 2, H, C), bf16),
            pltpu.VMEM((W, F, H, C), bf16),
            pltpu.VMEM((4, HALF * H, 3 * 256), f32),
            pltpu.VMEM((4, HALF * H, 128), f32),
            pltpu.VMEM((2, F, H, HALF, 256), bf16), pltpu.VMEM((2, F, H, HALF, 128), bf16),
            pltpu.VMEM((2, F, H, HALF, 256), bf16),
            dma((n,)), dma((n,)), dma((4,)), dma((4,)), dma(()), dma((9,)), dma(()), dma(()), dma((4,)),
        ],
        compiler_params=pltpu.CompilerParams(
            collective_id=0, has_side_effects=True, vmem_limit_bytes=44000000
        ),
        name="decoder_window",
    )(
        *(
            pltpu.with_memory_space_constraint(x, pltpu.HBM)
            for x in (
                latent, w_in.reshape(9, 3 * ZC, C), b_in, gain, w_mid.reshape(3, 3, 3 * C, C), b_mid,
                w_time.reshape(3 * C, 2 * C), b_time,
            )
        )
    )
    handed = [pltpu.with_memory_space_constraint(x, pltpu.VMEM) for x in handed]
    return pl.pallas_call(
        finish,
        out_shape=jax.ShapeDtypeStruct((2 * F, H, W, C), bf16),
        in_specs=[vmem] * 5,
        out_specs=hbm,
        scratch_shapes=[pltpu.VMEM((2 * F, H, HALF, C), bf16), dma((2, 2 * F))],
        compiler_params=pltpu.CompilerParams(vmem_limit_bytes=44000000),
        name="finish",
    )(*handed, b_time)


def solution(mesh):
    n = mesh.shape["tm"]
    return jax.shard_map(
        functools.partial(per_device, n),
        mesh=mesh,
        in_specs=(P("groups", "tm"), P(), P(), P(), P(), P(), P(), P()),
        out_specs=P(("groups", "tm"), None, None, None),
        check_vma=False,
    )
```

```python
import functools

import jax
import jax.numpy as jnp
from jax import lax
from jax.experimental import pallas as pl
from jax.experimental.pallas import tpu as pltpu
from jax.sharding import PartitionSpec as P

ZC = 16
C = 384
H = 16
W = 32
F = 2
ROW = W * ZC
WIDE = ROW + 128
GROUP = 4
HALF = W // 2
PARTS = ((0, 256), (256, 128))
MESH = pl.DeviceIdType.MESH


def kernel(
    n, latent_ref, w_in_ref, b_in_ref, gain_ref, w_mid_ref, b_mid_ref, w_time_ref, b_time_ref,
    part, halo_b, wtime, ready,
    b_in, gain, b_mid, b_time, mine, padded, sent, got, spread, rolled, win, band, wmid, mixed, hid, product, turn, own_a, own_b, halo_a,
    lat_send, lat_recv, halo_send, halo_recv, win_sem, wmid_sem, wtime_sem, mine_sem, vec_sem,
):
    bf16, f32 = jnp.bfloat16, jnp.float32
    me = lax.axis_index("tm")
    block = latent_ref.shape[1]
    frames = latent_ref.shape[0]
    per_row = ROW // block
    packed = sent.shape[2]

    mine_copy = pltpu.make_async_copy(latent_ref, mine, mine_sem)
    mine_copy.start()

    win_copy = pltpu.make_async_copy(w_in_ref, win, win_sem)
    vectors = ((b_in_ref, b_in), (gain_ref, gain), (b_mid_ref, b_mid), (b_time_ref, b_time))
    vec_copies = [
        pltpu.make_async_copy(src, dst, vec_sem.at[v]) for v, (src, dst) in enumerate(vectors)
    ]
    mid_copies = [
        [
            pltpu.make_async_copy(
                w_mid_ref.at[dt, di], wmid.at[(0, 1, 3)[dt], di], wmid_sem.at[di * 3 + dt]
            )
            for dt in range(3)
        ]
        for di in range(3)
    ]
    wtime_copy = pltpu.make_async_copy(w_time_ref, wtime, wtime_sem)

    def fetch():
        win_copy.start()
        for copy in vec_copies:
            copy.start()
        for copies in mid_copies:
            for copy in copies:
                copy.start()
        wtime_copy.start()

    barrier = pltpu.get_barrier_semaphore()

    def other(o):
        return lax.rem(me + o, n)

    quad = me - lax.rem(me, 4)
    first = [(c, k) for c in (3, 1, 2, 0)[:2] for k in range(1, n // 4)]
    last = [(c, k) for c in (3, 1, 2, 0)[2:] for k in range(1, n // 4)]
    targets = [lax.rem(quad + 4 * k + c, n) for c, k in first]
    targets += [quad + lax.rem(me + j, 4) for j in range(1, 4)]
    targets += [lax.rem(quad + 4 * k + c, n) for c, k in last]

    def greet(o, carry):
        pl.semaphore_signal(barrier, inc=1, device_id={"tm": other(o)}, device_id_type=MESH)
        return carry

    for o in range(1, n):
        greet(o, 0)
    fetch()

    padded[pl.ds(0, 8), :] = jnp.zeros((8, block), f32)
    padded[pl.ds(frames, 16), :] = jnp.zeros((16, block), f32)
    mine_copy.wait()
    padded[pl.ds(4, frames), :] = mine[...].astype(f32)
    for d in range(n):
        window = padded[pl.ds(F * d, 8), :]
        if packed < block:
            last = window[:, packed:]
            row = lax.broadcasted_iota(jnp.int32, (8, 128), 0)
            window = jnp.concatenate(
                [
                    jnp.where(
                        row < F + 4, window[:, c * 128 : (c + 1) * 128],
                        pltpu.roll(last, 6 - 2 * c, 0),
                    )
                    for c in range(3)
                ],
                axis=1,
            )
        sent[d] = window.astype(bf16)

    def combine(di):
        for copy in mid_copies[di]:
            copy.wait()

        def step(q, carry):
            here = (di, pl.ds(pl.multiple_of(q * 64, 64), 64))
            outer = wmid[0, *here].astype(f32) + wmid[3, *here].astype(f32)
            inner = wmid[1, *here].astype(f32)
            wmid[1, *here] = (outer + inner).astype(bf16)
            wmid[2, *here] = (outer - inner).astype(bf16)
            return carry

        lax.fori_loop(0, 3 * C // 64, step, 0)

    pl.semaphore_wait(barrier, n - 1)

    def lat_copy(d, j):
        return pltpu.make_async_remote_copy(
            src_ref=sent.at[d], dst_ref=got.at[j], send_sem=lat_send.at[d],
            recv_sem=lat_recv.at[j], device_id={"tm": d}, device_id_type=MESH,
        )

    for d in targets:
        lat_copy(d, me).start()

    def clear(t, carry):
        band[pl.ds(t * 128, 128), :] = jnp.zeros((128, GROUP * C), bf16)
        return carry

    lax.fori_loop(0, 8, clear, 0)
    for m in range(4):
        mixed[m, 0] = jnp.zeros((H, C), bf16)
        mixed[m, W + 1] = jnp.zeros((H, C), bf16)
    got[me] = sent[me]
    win_copy.wait()
    for c in range(GROUP):
        for t in range(8):
            band[pl.ds(t * 128 + ZC * c, 3 * ZC), pl.ds(c * C, C)] = win[t]
        for dj in range(3):
            third, odd = divmod(c + dj, 2)
            band[pl.ds(third * 128 + 96 + ZC * odd, ZC), pl.ds(c * C, C)] = win[8, pl.ds(ZC * dj, ZC)]
    for copy in vec_copies:
        copy.wait()

    for di in range(0, 3):
        combine(di)

    def receive(o, carry):
        lat_copy(other(o), other(o)).wait_recv()
        return carry

    for o in range(1, n):
        receive(o, 0)

    flat = got[...].astype(f32).reshape(n * 8, packed)
    for c in range(packed // 128):
        spread[c] = flat[:, c * 128 : (c + 1) * 128]
    picked = []
    for s in range(F + 4):
        parts = [
            spread[c, pl.ds(b * 8 + s, H, stride=8 * per_row), :]
            if c < packed // 128
            else spread[s // 2, pl.ds(b * 8 + 6 + s % 2, H, stride=8 * per_row), :]
            for b in range(per_row)
            for c in range(block // 128)
        ]
        parts.append(jnp.zeros((H, 128), f32))
        picked.append(jnp.concatenate(parts, axis=1))
    lat = jnp.concatenate(picked, axis=0)
    total = (F + 4) * H
    row_of = lax.broadcasted_iota(jnp.int32, (total, ROW), 0) & (H - 1)
    lane_of = lax.broadcasted_iota(jnp.int32, (total, ROW), 1) & 127
    for r in range(2):
        turned = pltpu.roll(lat, (ZC, WIDE - 3 * ZC)[r], 1)[:, :ROW]
        moved = (
            jnp.where(row_of == 0, 0.0, pltpu.roll(turned, 1, 0)),
            turned,
            jnp.where(row_of == H - 1, 0.0, pltpu.roll(turned, total - 1, 0)),
        )
        ninth = jnp.concatenate([moved[2][2 * H :], moved[2][: 2 * H]], axis=0)
        for di in range(3):
            third = pltpu.roll(ninth, 96 - 32 * di, 1)
            rolled[r, di] = jnp.where(lane_of < 96, moved[di], third).astype(bf16)

    wide = (F + 2) * H
    keep = jnp.where(me > 0, 1.0, 0.0)

    def columns(r, carry):
        left = jnp.concatenate(
            [
                jnp.concatenate(
                    [
                        rolled[r, t % 3, pl.ds((t // 3) * H, wide), pl.ds(128 * b, 128)]
                        for b in range(4)
                    ],
                    axis=0,
                )
                for t in range(8)
            ],
            axis=1,
        )
        for pair in range(2):
            both = jnp.dot(
                left, band[:, pl.ds(pair * 2 * C, 2 * C)], preferred_element_type=f32
            )
            for c in range(2):
                h0 = (both[:, c * C : (c + 1) * C] + b_in[...][None, :]).astype(bf16)
                values = h0.astype(f32)
                scale = lax.rsqrt(jnp.mean(values * values, axis=-1, keepdims=True) + 1e-06)
                half = values * (0.5 * scale) * gain[...][None, :]
                act = half + half * jnp.tanh(half)
                for b in range(4):
                    w = 8 * b + 4 * r + 2 * pair + c
                    d0, d1, d2, d3 = (
                        act[b * wide + f * H : b * wide + (f + 1) * H] for f in range(4)
                    )
                    d0, d1 = d0 * keep, d1 * keep
                    mixed[0, w + 1] = (d0 - d2).astype(bf16)
                    mixed[1, w + 1] = (0.5 * (d1 + d2)).astype(bf16)
                    mixed[2, w + 1] = (0.5 * (d2 - d1)).astype(bf16)
                    mixed[3, w + 1] = (d1 - d3).astype(bf16)
                    for a in range(F):
                        hid[w, a] = h0[b * wide + (a + 2) * H : b * wide + (a + 3) * H]
        return carry

    for r in range(2):
        columns(r, 0)

    after = lax.rem(me + 1, n)

    own, halo = (own_a, own_b), (halo_a, halo_b)

    def halo_copy(h, p):
        return pltpu.make_async_remote_copy(
            src_ref=own[p].at[h], dst_ref=halo[p].at[h],
            send_sem=halo_send.at[h * 2 + p], recv_sem=halo_recv.at[h * 2 + p],
            device_id={"tm": after}, device_id_type=MESH,
        )

    rows = HALF * H

    def residual(h, carry):
        w0 = pl.multiple_of(h * HALF, HALF)
        for p, (c0, width) in enumerate(PARTS):
            for m in range(4):
                left = jnp.concatenate(
                    [mixed[m, pl.ds(w0 + dj, HALF)].reshape(rows, C) for dj in range(3)], axis=1
                )
                product[m, :, pl.ds(0, 3 * width)] = jnp.dot(
                    left,
                    jnp.concatenate(
                        [wmid[m, di, :, pl.ds(c0, width)] for di in range(3)], axis=1
                    ),
                    preferred_element_type=f32,
                )
            p0, p1, p2, p3 = (product[m, :, pl.ds(0, 3 * width)] for m in range(4))
            row = lax.broadcasted_iota(jnp.int32, (rows, width), 0) & (H - 1)
            for f, three in enumerate((p0 + p1 + p2, p1 - p2 - p3)):
                above = pltpu.roll(three[:, :width], 1, 0)
                below = pltpu.roll(three[:, 2 * width :], rows - 1, 0)
                acc = hid[pl.ds(w0, HALF), f, :, pl.ds(c0, width)].astype(f32).reshape(rows, width)
                acc = acc + b_mid[pl.ds(c0, width)][None, :] + three[:, width : 2 * width]
                acc = acc + jnp.where(row == 0, 0.0, above) + jnp.where(row == H - 1, 0.0, below)
                for c in range(width // 128):
                    turn[f * 2 + c] = acc[:, c * 128 : (c + 1) * 128]
                for i in range(H):
                    line = [
                        turn[f * 2 + c, pl.ds(i, HALF, stride=H), :] for c in range(width // 128)
                    ]
                    own[p][h, f, i] = jnp.concatenate(
                        line, axis=1
                    ).astype(bf16)

            @pl.when(me < n - 1)
            def _():
                halo_copy(h, p).start()

        return carry

    lax.fori_loop(0, 2, residual, 0)

    wtime_copy.wait()

    def both(pair, h, f):
        return jnp.concatenate(
            [ref[h, f].reshape(rows, width) for ref, (_, width) in zip(pair, PARTS)], axis=1
        )

    for h in range(2):
        mine0, mine1 = (both(own, h, f) for f in range(F))
        part[0, h] = jnp.dot(mine0, wtime[pl.ds(2 * C, C)], preferred_element_type=f32)
        part[1, h] = jnp.dot(
            jnp.concatenate([mine0, mine1], axis=1), wtime[pl.ds(C, 2 * C)],
            preferred_element_type=f32,
        )

    def sent_all(o, carry):
        lat_copy(other(o), me).wait_send()
        return carry

    lax.fori_loop(1, n, sent_all, 0)

    def gather(h, p):
        halo_copy(h, p).wait_recv()
        if (h, p) != (1, 1):
            c0, width = PARTS[p]
            past0, past1 = (halo[p][h, f].reshape(rows, width) for f in range(F))
            part[0, h] += jnp.dot(
                jnp.concatenate([past0, past1], axis=1),
                jnp.concatenate([wtime[pl.ds(f * C + c0, width)] for f in range(F)], axis=0),
                preferred_element_type=f32,
            )
            part[1, h] += jnp.dot(past1, wtime[pl.ds(c0, width)], preferred_element_type=f32)

    @pl.when(me > 0)
    def _():
        gather(0, 0)
        gather(0, 1)

    for f in range(F):
        up = (part[f, 0] + b_time[...][None, :]).astype(bf16)
        for s in range(2):
            ready[2 * f + s] = up[:, s * C : (s + 1) * C].reshape(H, HALF, C)

    @pl.when(me > 0)
    def _():
        gather(1, 0)
        gather(1, 1)

    @pl.when(me == 0)
    def _():
        halo_b[1] = jnp.zeros(halo_b.shape[1:], bf16)

    @pl.when(me < n - 1)
    def _():
        for h in range(2):
            for p in range(2):
                halo_copy(h, p).wait_send()


def finish(part, halo_b, wtime, ready, b_time, out_ref, staged, out_sem):
    rows = HALF * H

    def out_copy(h, e):
        return pltpu.make_async_copy(
            (ready, staged)[h].at[e], out_ref.at[e, :, pl.ds(h * HALF, HALF)], out_sem.at[h, e]
        )

    def put(h, f, up):
        up = (up + b_time[...][None, :]).astype(jnp.bfloat16)
        for s in range(2):
            staged[2 * f + s] = up[:, s * C : (s + 1) * C].reshape(H, HALF, C)
            out_copy(h, 2 * f + s).start()

    for e in range(2 * F):
        out_copy(0, e).start()
    c0, width = PARTS[1]
    past0, past1 = (halo_b[1, f].reshape(rows, width) for f in range(F))
    put(
        1, 0,
        part[0, 1]
        + jnp.dot(
            jnp.concatenate([past0, past1], axis=1),
            jnp.concatenate([wtime[pl.ds(f * C + c0, width)] for f in range(F)], axis=0),
            preferred_element_type=jnp.float32,
        ),
    )
    put(
        1, 1,
        part[1, 1]
        + jnp.dot(past1, wtime[pl.ds(c0, width)], preferred_element_type=jnp.float32),
    )
    for h in range(2):
        for e in range(2 * F):
            out_copy(h, e).wait()


def per_device(n, latent, w_in, b_in, gain, w_mid, b_mid, w_time, b_time):
    frames, block = latent.shape
    assert frames == F * n
    bf16, f32 = jnp.bfloat16, jnp.float32
    packed = block * 3 // 4 if block == 512 else block
    vmem = pl.BlockSpec(memory_space=pltpu.VMEM)
    hbm = pl.BlockSpec(memory_space=pltpu.HBM)
    dma = pltpu.SemaphoreType.DMA
    handed = pl.pallas_call(
        functools.partial(kernel, n),
        out_shape=(
            pltpu.VMEM((F, 2, HALF * H, 2 * C), f32),
            pltpu.VMEM((2, F, H, HALF, 128), bf16),
            pltpu.VMEM((3 * C, 2 * C), bf16),
            pltpu.VMEM((2 * F, H, HALF, C), bf16),
        ),
        in_specs=[hbm] * 8,
        out_specs=[vmem] * 4,
        scratch_shapes=[
            pltpu.VMEM((C,), f32), pltpu.VMEM((C,), f32), pltpu.VMEM((C,), f32),
            pltpu.VMEM((2 * C,), f32),
            pltpu.VMEM((frames, block), bf16),
            pltpu.VMEM((frames + 16, block), f32),
            pltpu.VMEM((n, 8, packed), bf16),
            pltpu.VMEM((n, 8, packed), bf16),
            pltpu.VMEM((block // 128, n * 8, 128), f32),
            pltpu.VMEM((2, 3, (F + 4) * H, ROW), bf16),
            pltpu.VMEM((9, 3 * ZC, C), bf16),
            pltpu.VMEM((8 * 128, GROUP * C), bf16),
            pltpu.VMEM((4, 3, 3 * C, C), bf16),
            pltpu.VMEM((4, W + 2, H, C), bf16),
            pltpu.VMEM((W, F, H, C), bf16),
            pltpu.VMEM((4, HALF * H, 3 * 256), f32),
            pltpu.VMEM((4, HALF * H, 128), f32),
            pltpu.VMEM((2, F, H, HALF, 256), bf16), pltpu.VMEM((2, F, H, HALF, 128), bf16),
            pltpu.VMEM((2, F, H, HALF, 256), bf16),
            dma((n,)), dma((n,)), dma((4,)), dma((4,)), dma(()), dma((9,)), dma(()), dma(()), dma((4,)),
        ],
        compiler_params=pltpu.CompilerParams(
            collective_id=0, has_side_effects=True, vmem_limit_bytes=44000000
        ),
        name="decoder_window",
    )(
        *(
            pltpu.with_memory_space_constraint(x, pltpu.HBM)
            for x in (
                latent, w_in.reshape(9, 3 * ZC, C), b_in, gain, w_mid.reshape(3, 3, 3 * C, C), b_mid,
                w_time.reshape(3 * C, 2 * C), b_time,
            )
        )
    )
    handed = [pltpu.with_memory_space_constraint(x, pltpu.VMEM) for x in handed]
    return pl.pallas_call(
        finish,
        out_shape=jax.ShapeDtypeStruct((2 * F, H, W, C), bf16),
        in_specs=[vmem] * 5,
        out_specs=hbm,
        scratch_shapes=[pltpu.VMEM((2 * F, H, HALF, C), bf16), dma((2, 2 * F))],
        compiler_params=pltpu.CompilerParams(vmem_limit_bytes=44000000),
        name="finish",
    )(*handed, b_time)


def solution(mesh):
    n = mesh.shape["tm"]
    return jax.shard_map(
        functools.partial(per_device, n),
        mesh=mesh,
        in_specs=(P("groups", "tm"), P(), P(), P(), P(), P(), P(), P()),
        out_specs=P(("groups", "tm"), None, None, None),
        check_vma=False,
    )
```

```python
import functools

import jax
import jax.numpy as jnp
from jax import lax
from jax.experimental import pallas as pl
from jax.experimental.pallas import tpu as pltpu
from jax.sharding import PartitionSpec as P

ZC = 16
C = 384
H = 16
W = 32
F = 2
ROW = W * ZC
WIDE = ROW + 128
GROUP = 4
HALF = W // 2
PARTS = ((0, 256), (256, 128))
MESH = pl.DeviceIdType.MESH


def kernel(
    n, latent_ref, w_in_ref, b_in_ref, gain_ref, w_mid_ref, b_mid_ref, w_time_ref, b_time_ref,
    part, halo_b, wtime, ready,
    b_in, gain, b_mid, b_time, mine, padded, sent, got, spread, rolled, win, band, wmid, mixed, hid, product, turn, own_a, own_b, halo_a,
    lat_send, lat_recv, halo_send, halo_recv, win_sem, wmid_sem, wtime_sem, mine_sem, vec_sem,
):
    bf16, f32 = jnp.bfloat16, jnp.float32
    me = lax.axis_index("tm")
    block = latent_ref.shape[1]
    frames = latent_ref.shape[0]
    per_row = ROW // block
    packed = sent.shape[2]

    mine_copy = pltpu.make_async_copy(latent_ref, mine, mine_sem)
    mine_copy.start()

    win_copy = pltpu.make_async_copy(w_in_ref, win, win_sem)
    vectors = ((b_in_ref, b_in), (gain_ref, gain), (b_mid_ref, b_mid), (b_time_ref, b_time))
    vec_copies = [
        pltpu.make_async_copy(src, dst, vec_sem.at[v]) for v, (src, dst) in enumerate(vectors)
    ]
    mid_copies = [
        [
            pltpu.make_async_copy(
                w_mid_ref.at[dt, di], wmid.at[(0, 1, 3)[dt], di], wmid_sem.at[di * 3 + dt]
            )
            for dt in range(3)
        ]
        for di in range(3)
    ]
    wtime_copy = pltpu.make_async_copy(w_time_ref, wtime, wtime_sem)

    def fetch():
        win_copy.start()
        for copy in vec_copies:
            copy.start()
        for copies in mid_copies:
            for copy in copies:
                copy.start()
        wtime_copy.start()

    barrier = pltpu.get_barrier_semaphore()

    def other(o):
        return lax.rem(me + o, n)

    quad = me - lax.rem(me, 4)
    last = [(c, k) for c in (3, 1, 2, 0)[2:] for k in range(1, n // 4)]
    ones = [4 * (k + jnp.where(4 * k >= quad, 1, 0)) + 1 for k in range(n // 4 - 1)]
    targets = ones[:1] + [lax.rem(quad + 4 * k + 3, n) for k in range(1, n // 4)] + ones[1:]
    targets += [quad + lax.rem(me + j, 4) for j in range(1, 4)]
    targets += [lax.rem(quad + 4 * k + c, n) for c, k in last]

    def greet(o, carry):
        pl.semaphore_signal(barrier, inc=1, device_id={"tm": other(o)}, device_id_type=MESH)
        return carry

    for o in range(1, n):
        greet(o, 0)
    fetch()

    padded[pl.ds(0, 8), :] = jnp.zeros((8, block), f32)
    padded[pl.ds(frames, 16), :] = jnp.zeros((16, block), f32)
    mine_copy.wait()
    padded[pl.ds(4, frames), :] = mine[...].astype(f32)
    for d in range(n):
        window = padded[pl.ds(F * d, 8), :]
        if packed < block:
            last = window[:, packed:]
            row = lax.broadcasted_iota(jnp.int32, (8, 128), 0)
            window = jnp.concatenate(
                [
                    jnp.where(
                        row < F + 4, window[:, c * 128 : (c + 1) * 128],
                        pltpu.roll(last, 6 - 2 * c, 0),
                    )
                    for c in range(3)
                ],
                axis=1,
            )
        sent[d] = window.astype(bf16)

    def combine(di):
        for copy in mid_copies[di]:
            copy.wait()

        def step(q, carry):
            here = (di, pl.ds(pl.multiple_of(q * 64, 64), 64))
            outer = wmid[0, *here].astype(f32) + wmid[3, *here].astype(f32)
            inner = wmid[1, *here].astype(f32)
            wmid[1, *here] = (outer + inner).astype(bf16)
            wmid[2, *here] = (outer - inner).astype(bf16)
            return carry

        lax.fori_loop(0, 3 * C // 64, step, 0)

    pl.semaphore_wait(barrier, n - 1)

    def lat_copy(d, j):
        return pltpu.make_async_remote_copy(
            src_ref=sent.at[d], dst_ref=got.at[j], send_sem=lat_send.at[d],
            recv_sem=lat_recv.at[j], device_id={"tm": d}, device_id_type=MESH,
        )

    for d in targets:
        lat_copy(d, me).start()

    def clear(t, carry):
        band[pl.ds(t * 128, 128), :] = jnp.zeros((128, GROUP * C), bf16)
        return carry

    lax.fori_loop(0, 8, clear, 0)
    for m in range(4):
        mixed[m, 0] = jnp.zeros((H, C), bf16)
        mixed[m, W + 1] = jnp.zeros((H, C), bf16)
    got[me] = sent[me]
    win_copy.wait()
    for c in range(GROUP):
        for t in range(8):
            band[pl.ds(t * 128 + ZC * c, 3 * ZC), pl.ds(c * C, C)] = win[t]
        for dj in range(3):
            third, odd = divmod(c + dj, 2)
            band[pl.ds(third * 128 + 96 + ZC * odd, ZC), pl.ds(c * C, C)] = win[8, pl.ds(ZC * dj, ZC)]
    for copy in vec_copies:
        copy.wait()

    for di in range(0, 3):
        combine(di)

    def receive(o, carry):
        lat_copy(other(o), other(o)).wait_recv()
        return carry

    for o in range(1, n):
        receive(o, 0)

    flat = got[...].astype(f32).reshape(n * 8, packed)
    for c in range(packed // 128):
        spread[c] = flat[:, c * 128 : (c + 1) * 128]
    picked = []
    for s in range(F + 4):
        parts = [
            spread[c, pl.ds(b * 8 + s, H, stride=8 * per_row), :]
            if c < packed // 128
            else spread[s // 2, pl.ds(b * 8 + 6 + s % 2, H, stride=8 * per_row), :]
            for b in range(per_row)
            for c in range(block // 128)
        ]
        parts.append(jnp.zeros((H, 128), f32))
        picked.append(jnp.concatenate(parts, axis=1))
    lat = jnp.concatenate(picked, axis=0)
    total = (F + 4) * H
    row_of = lax.broadcasted_iota(jnp.int32, (total, ROW), 0) & (H - 1)
    lane_of = lax.broadcasted_iota(jnp.int32, (total, ROW), 1) & 127
    for r in range(2):
        turned = pltpu.roll(lat, (ZC, WIDE - 3 * ZC)[r], 1)[:, :ROW]
        moved = (
            jnp.where(row_of == 0, 0.0, pltpu.roll(turned, 1, 0)),
            turned,
            jnp.where(row_of == H - 1, 0.0, pltpu.roll(turned, total - 1, 0)),
        )
        ninth = jnp.concatenate([moved[2][2 * H :], moved[2][: 2 * H]], axis=0)
        for di in range(3):
            third = pltpu.roll(ninth, 96 - 32 * di, 1)
            rolled[r, di] = jnp.where(lane_of < 96, moved[di], third).astype(bf16)

    wide = (F + 2) * H
    keep = jnp.where(me > 0, 1.0, 0.0)

    def columns(r, carry):
        left = jnp.concatenate(
            [
                jnp.concatenate(
                    [
                        rolled[r, t % 3, pl.ds((t // 3) * H, wide), pl.ds(128 * b, 128)]
                        for b in range(4)
                    ],
                    axis=0,
                )
                for t in range(8)
            ],
            axis=1,
        )
        for pair in range(2):
            both = jnp.dot(
                left, band[:, pl.ds(pair * 2 * C, 2 * C)], preferred_element_type=f32
            )
            for c in range(2):
                h0 = (both[:, c * C : (c + 1) * C] + b_in[...][None, :]).astype(bf16)
                values = h0.astype(f32)
                scale = lax.rsqrt(jnp.mean(values * values, axis=-1, keepdims=True) + 1e-06)
                half = values * (0.5 * scale) * gain[...][None, :]
                act = half + half * jnp.tanh(half)
                for b in range(4):
                    w = 8 * b + 4 * r + 2 * pair + c
                    d0, d1, d2, d3 = (
                        act[b * wide + f * H : b * wide + (f + 1) * H] for f in range(4)
                    )
                    d0, d1 = d0 * keep, d1 * keep
                    mixed[0, w + 1] = (d0 - d2).astype(bf16)
                    mixed[1, w + 1] = (0.5 * (d1 + d2)).astype(bf16)
                    mixed[2, w + 1] = (0.5 * (d2 - d1)).astype(bf16)
                    mixed[3, w + 1] = (d1 - d3).astype(bf16)
                    for a in range(F):
                        hid[w, a] = h0[b * wide + (a + 2) * H : b * wide + (a + 3) * H]
        return carry

    for r in range(2):
        columns(r, 0)

    after = lax.rem(me + 1, n)

    own, halo = (own_a, own_b), (halo_a, halo_b)

    def halo_copies(h, p):
        slots = [(h * 3 + f, (h, f)) for f in range(F)] if p == 0 else [(h * 3 + 2, (h,))]
        return [
            pltpu.make_async_remote_copy(
                src_ref=own[p].at[here], dst_ref=halo[p].at[here],
                send_sem=halo_send.at[slot], recv_sem=halo_recv.at[slot],
                device_id={"tm": after}, device_id_type=MESH,
            )
            for slot, here in slots
        ]

    rows = HALF * H

    def residual(h, carry):
        w0 = pl.multiple_of(h * HALF, HALF)
        for p, (c0, width) in enumerate(PARTS):
            def multiply(m, c0=c0, width=width):
                left = jnp.concatenate(
                    [mixed[m, pl.ds(w0 + dj, HALF)].reshape(rows, C) for dj in range(3)], axis=1
                )
                product[m, :, pl.ds(0, 3 * width)] = jnp.dot(
                    left,
                    jnp.concatenate(
                        [wmid[m, di, :, pl.ds(c0, width)] for di in range(3)], axis=1
                    ),
                    preferred_element_type=f32,
                )

            split = p == 0
            row = lax.broadcasted_iota(jnp.int32, (rows, width), 0) & (H - 1)
            for f in range(F):
                for m in ((1, 2, 0), (3,))[f] if split else ((1, 2, 0, 3), ())[f]:
                    multiply(m)
                p0, p1, p2, p3 = (product[m, :, pl.ds(0, 3 * width)] for m in range(4))
                three = p0 + p1 + p2 if f == 0 else p1 - p2 - p3
                above = pltpu.roll(three[:, :width], 1, 0)
                below = pltpu.roll(three[:, 2 * width :], rows - 1, 0)
                acc = hid[pl.ds(w0, HALF), f, :, pl.ds(c0, width)].astype(f32).reshape(rows, width)
                acc = acc + b_mid[pl.ds(c0, width)][None, :] + three[:, width : 2 * width]
                acc = acc + jnp.where(row == 0, 0.0, above) + jnp.where(row == H - 1, 0.0, below)
                for c in range(width // 128):
                    turn[f * 2 + c] = acc[:, c * 128 : (c + 1) * 128]
                for i in range(H):
                    line = [
                        turn[f * 2 + c, pl.ds(i, HALF, stride=H), :] for c in range(width // 128)
                    ]
                    own[p][h, f, i] = jnp.concatenate(
                        line, axis=1
                    ).astype(bf16)

                if split or f == F - 1:
                    @pl.when(me < n - 1)
                    def _():
                        for copy in halo_copies(h, p)[f if split else 0 :][:1]:
                            copy.start()

        return carry

    lax.fori_loop(0, 2, residual, 0)

    wtime_copy.wait()

    def both(pair, h, f):
        return jnp.concatenate(
            [ref[h, f].reshape(rows, width) for ref, (_, width) in zip(pair, PARTS)], axis=1
        )

    for h in range(2):
        mine0, mine1 = (both(own, h, f) for f in range(F))
        part[0, h] = jnp.dot(mine0, wtime[pl.ds(2 * C, C)], preferred_element_type=f32)
        part[1, h] = jnp.dot(
            jnp.concatenate([mine0, mine1], axis=1), wtime[pl.ds(C, 2 * C)],
            preferred_element_type=f32,
        )

    def sent_all(o, carry):
        lat_copy(other(o), me).wait_send()
        return carry

    lax.fori_loop(1, n, sent_all, 0)

    def gather(h, p):
        for copy in halo_copies(h, p):
            copy.wait_recv()
        if (h, p) != (1, 1):
            c0, width = PARTS[p]
            past0, past1 = (halo[p][h, f].reshape(rows, width) for f in range(F))
            part[0, h] += jnp.dot(
                jnp.concatenate([past0, past1], axis=1),
                jnp.concatenate([wtime[pl.ds(f * C + c0, width)] for f in range(F)], axis=0),
                preferred_element_type=f32,
            )
            part[1, h] += jnp.dot(past1, wtime[pl.ds(c0, width)], preferred_element_type=f32)

    @pl.when(me > 0)
    def _():
        gather(0, 0)
        gather(0, 1)

    for f in range(F):
        up = (part[f, 0] + b_time[...][None, :]).astype(bf16)
        for s in range(2):
            ready[2 * f + s] = up[:, s * C : (s + 1) * C].reshape(H, HALF, C)

    @pl.when(me > 0)
    def _():
        gather(1, 0)
        gather(1, 1)

    @pl.when(me == 0)
    def _():
        halo_b[1] = jnp.zeros(halo_b.shape[1:], bf16)

    @pl.when(me < n - 1)
    def _():
        for h in range(2):
            for p in range(2):
                for copy in halo_copies(h, p):
                    copy.wait_send()


def finish(part, halo_b, wtime, ready, b_time, out_ref, staged, out_sem):
    rows = HALF * H

    def out_copy(h, e):
        return pltpu.make_async_copy(
            (ready, staged)[h].at[e], out_ref.at[e, :, pl.ds(h * HALF, HALF)], out_sem.at[h, e]
        )

    def put(h, f, up):
        up = (up + b_time[...][None, :]).astype(jnp.bfloat16)
        for s in range(2):
            staged[2 * f + s] = up[:, s * C : (s + 1) * C].reshape(H, HALF, C)
            out_copy(h, 2 * f + s).start()

    for e in range(2 * F):
        out_copy(0, e).start()
    c0, width = PARTS[1]
    past0, past1 = (halo_b[1, f].reshape(rows, width) for f in range(F))
    put(
        1, 0,
        part[0, 1]
        + jnp.dot(
            jnp.concatenate([past0, past1], axis=1),
            jnp.concatenate([wtime[pl.ds(f * C + c0, width)] for f in range(F)], axis=0),
            preferred_element_type=jnp.float32,
        ),
    )
    put(
        1, 1,
        part[1, 1]
        + jnp.dot(past1, wtime[pl.ds(c0, width)], preferred_element_type=jnp.float32),
    )
    for h in range(2):
        for e in range(2 * F):
            out_copy(h, e).wait()


def per_device(n, latent, w_in, b_in, gain, w_mid, b_mid, w_time, b_time):
    frames, block = latent.shape
    assert frames == F * n
    bf16, f32 = jnp.bfloat16, jnp.float32
    packed = block * 3 // 4 if block == 512 else block
    vmem = pl.BlockSpec(memory_space=pltpu.VMEM)
    hbm = pl.BlockSpec(memory_space=pltpu.HBM)
    dma = pltpu.SemaphoreType.DMA
    handed = pl.pallas_call(
        functools.partial(kernel, n),
        out_shape=(
            pltpu.VMEM((F, 2, HALF * H, 2 * C), f32),
            pltpu.VMEM((2, F, H, HALF, 128), bf16),
            pltpu.VMEM((3 * C, 2 * C), bf16),
            pltpu.VMEM((2 * F, H, HALF, C), bf16),
        ),
        in_specs=[hbm] * 8,
        out_specs=[vmem] * 4,
        scratch_shapes=[
            pltpu.VMEM((C,), f32), pltpu.VMEM((C,), f32), pltpu.VMEM((C,), f32),
            pltpu.VMEM((2 * C,), f32),
            pltpu.VMEM((frames, block), bf16),
            pltpu.VMEM((frames + 16, block), f32),
            pltpu.VMEM((n, 8, packed), bf16),
            pltpu.VMEM((n, 8, packed), bf16),
            pltpu.VMEM((block // 128, n * 8, 128), f32),
            pltpu.VMEM((2, 3, (F + 4) * H, ROW), bf16),
            pltpu.VMEM((9, 3 * ZC, C), bf16),
            pltpu.VMEM((8 * 128, GROUP * C), bf16),
            pltpu.VMEM((4, 3, 3 * C, C), bf16),
            pltpu.VMEM((4, W + 2, H, C), bf16),
            pltpu.VMEM((W, F, H, C), bf16),
            pltpu.VMEM((4, HALF * H, 3 * 256), f32),
            pltpu.VMEM((4, HALF * H, 128), f32),
            pltpu.VMEM((2, F, H, HALF, 256), bf16), pltpu.VMEM((2, F, H, HALF, 128), bf16),
            pltpu.VMEM((2, F, H, HALF, 256), bf16),
            dma((n,)), dma((n,)), dma((6,)), dma((6,)), dma(()), dma((9,)), dma(()), dma(()), dma((4,)),
        ],
        compiler_params=pltpu.CompilerParams(
            collective_id=0, has_side_effects=True, vmem_limit_bytes=44000000
        ),
        name="decoder_window",
    )(
        *(
            pltpu.with_memory_space_constraint(x, pltpu.HBM)
            for x in (
                latent, w_in.reshape(9, 3 * ZC, C), b_in, gain, w_mid.reshape(3, 3, 3 * C, C), b_mid,
                w_time.reshape(3 * C, 2 * C), b_time,
            )
        )
    )
    handed = [pltpu.with_memory_space_constraint(x, pltpu.VMEM) for x in handed]
    return pl.pallas_call(
        finish,
        out_shape=jax.ShapeDtypeStruct((2 * F, H, W, C), bf16),
        in_specs=[vmem] * 5,
        out_specs=hbm,
        scratch_shapes=[pltpu.VMEM((2 * F, H, HALF, C), bf16), dma((2, 2 * F))],
        compiler_params=pltpu.CompilerParams(vmem_limit_bytes=44000000),
        name="finish",
    )(*handed, b_time)


def solution(mesh):
    n = mesh.shape["tm"]
    return jax.shard_map(
        functools.partial(per_device, n),
        mesh=mesh,
        in_specs=(P("groups", "tm"), P(), P(), P(), P(), P(), P(), P()),
        out_specs=P(("groups", "tm"), None, None, None),
        check_vma=False,
    )
```

```python
import functools

import jax
import jax.numpy as jnp
from jax import lax
from jax.experimental import pallas as pl
from jax.experimental.pallas import tpu as pltpu
from jax.sharding import PartitionSpec as P

ZC = 16
C = 384
H = 16
W = 32
F = 2
ROW = W * ZC
WIDE = ROW + 128
GROUP = 4
HALF = W // 2
PARTS = ((0, 256), (256, 128))
MESH = pl.DeviceIdType.MESH


def kernel(
    n, latent_ref, w_in_ref, b_in_ref, gain_ref, w_mid_ref, b_mid_ref, w_time_ref, b_time_ref,
    part, halo_b, wtime, ready,
    b_in, gain, b_mid, b_time, mine, padded, sent, got, spread, rolled, win, band, wmid, mixed, hid, product, turn, own_a, own_b, halo_a,
    lat_send, lat_recv, halo_send, halo_recv, win_sem, wmid_sem, wtime_sem, mine_sem, vec_sem,
):
    bf16, f32 = jnp.bfloat16, jnp.float32
    me = lax.axis_index("tm")
    block = latent_ref.shape[1]
    frames = latent_ref.shape[0]
    per_row = ROW // block
    packed = sent.shape[2]

    mine_copy = pltpu.make_async_copy(latent_ref, mine, mine_sem)
    mine_copy.start()

    win_copy = pltpu.make_async_copy(w_in_ref, win, win_sem)
    vectors = ((b_in_ref, b_in), (gain_ref, gain), (b_mid_ref, b_mid), (b_time_ref, b_time))
    vec_copies = [
        pltpu.make_async_copy(src, dst, vec_sem.at[v]) for v, (src, dst) in enumerate(vectors)
    ]
    mid_copies = [
        [
            pltpu.make_async_copy(
                w_mid_ref.at[dt, di], wmid.at[(0, 1, 3)[dt], di], wmid_sem.at[di * 3 + dt]
            )
            for dt in range(3)
        ]
        for di in range(3)
    ]
    wtime_copy = pltpu.make_async_copy(w_time_ref, wtime, wtime_sem)

    def fetch():
        win_copy.start()
        for copy in vec_copies:
            copy.start()
        for copies in mid_copies:
            for copy in copies:
                copy.start()
        wtime_copy.start()

    barrier = pltpu.get_barrier_semaphore()

    def other(o):
        return lax.rem(me + o, n)

    quad = me - lax.rem(me, 4)
    last = [(c, k) for c in (3, 1, 2, 0)[2:] for k in range(1, n // 4)]
    ones = [4 * (k + jnp.where(4 * k >= quad, 1, 0)) + 1 for k in range(n // 4 - 1)]
    targets = ones[:1] + [lax.rem(quad + 4 * k + 3, n) for k in range(1, n // 4)] + ones[1:]
    targets += [quad + lax.rem(me + j, 4) for j in range(1, 4)]
    targets += [lax.rem(quad + 4 * k + c, n) for c, k in last]

    def greet(o, carry):
        pl.semaphore_signal(barrier, inc=1, device_id={"tm": other(o)}, device_id_type=MESH)
        return carry

    for o in range(1, n):
        greet(o, 0)
    fetch()

    padded[pl.ds(0, 8), :] = jnp.zeros((8, block), f32)
    padded[pl.ds(frames, 16), :] = jnp.zeros((16, block), f32)
    mine_copy.wait()
    padded[pl.ds(4, frames), :] = mine[...].astype(f32)
    for d in range(n):
        window = padded[pl.ds(F * d, 8), :]
        if packed < block:
            last = window[:, packed:]
            row = lax.broadcasted_iota(jnp.int32, (8, 128), 0)
            window = jnp.concatenate(
                [
                    jnp.where(
                        row < F + 4, window[:, c * 128 : (c + 1) * 128],
                        pltpu.roll(last, 6 - 2 * c, 0),
                    )
                    for c in range(3)
                ],
                axis=1,
            )
        sent[d] = window.astype(bf16)

    def combine(di):
        for copy in mid_copies[di]:
            copy.wait()

        def step(q, carry):
            here = (di, pl.ds(pl.multiple_of(q * 64, 64), 64))
            outer = wmid[0, *here].astype(f32) + wmid[3, *here].astype(f32)
            inner = wmid[1, *here].astype(f32)
            wmid[1, *here] = (outer + inner).astype(bf16)
            wmid[2, *here] = (outer - inner).astype(bf16)
            return carry

        lax.fori_loop(0, 3 * C // 64, step, 0)

    pl.semaphore_wait(barrier, n - 1)

    def lat_copy(d, j):
        return pltpu.make_async_remote_copy(
            src_ref=sent.at[d], dst_ref=got.at[j], send_sem=lat_send.at[d],
            recv_sem=lat_recv.at[j], device_id={"tm": d}, device_id_type=MESH,
        )

    for d in targets:
        lat_copy(d, me).start()

    def clear(t, carry):
        band[pl.ds(t * 128, 128), :] = jnp.zeros((128, GROUP * C), bf16)
        return carry

    lax.fori_loop(0, 8, clear, 0)
    for m in range(4):
        mixed[m, 0] = jnp.zeros((H, C), bf16)
        mixed[m, W + 1] = jnp.zeros((H, C), bf16)
    got[me] = sent[me]
    win_copy.wait()
    for c in range(GROUP):
        for t in range(8):
            band[pl.ds(t * 128 + ZC * c, 3 * ZC), pl.ds(c * C, C)] = win[t]
        for dj in range(3):
            third, odd = divmod(c + dj, 2)
            band[pl.ds(third * 128 + 96 + ZC * odd, ZC), pl.ds(c * C, C)] = win[8, pl.ds(ZC * dj, ZC)]
    for copy in vec_copies:
        copy.wait()

    for di in range(0, 3):
        combine(di)

    def receive(o, carry):
        lat_copy(other(o), other(o)).wait_recv()
        return carry

    for o in range(1, n):
        receive(o, 0)

    flat = got[...].astype(f32).reshape(n * 8, packed)
    for c in range(packed // 128):
        spread[c] = flat[:, c * 128 : (c + 1) * 128]
    picked = []
    for s in range(F + 4):
        parts = [
            spread[c, pl.ds(b * 8 + s, H, stride=8 * per_row), :]
            if c < packed // 128
            else spread[s // 2, pl.ds(b * 8 + 6 + s % 2, H, stride=8 * per_row), :]
            for b in range(per_row)
            for c in range(block // 128)
        ]
        parts.append(jnp.zeros((H, 128), f32))
        picked.append(jnp.concatenate(parts, axis=1))
    lat = jnp.concatenate(picked, axis=0)
    total = (F + 4) * H
    row_of = lax.broadcasted_iota(jnp.int32, (total, ROW), 0) & (H - 1)
    lane_of = lax.broadcasted_iota(jnp.int32, (total, ROW), 1) & 127
    for r in range(2):
        turned = pltpu.roll(lat, (ZC, WIDE - 3 * ZC)[r], 1)[:, :ROW]
        moved = (
            jnp.where(row_of == 0, 0.0, pltpu.roll(turned, 1, 0)),
            turned,
            jnp.where(row_of == H - 1, 0.0, pltpu.roll(turned, total - 1, 0)),
        )
        ninth = jnp.concatenate([moved[2][2 * H :], moved[2][: 2 * H]], axis=0)
        for di in range(3):
            third = pltpu.roll(ninth, 96 - 32 * di, 1)
            rolled[r, di] = jnp.where(lane_of < 96, moved[di], third).astype(bf16)

    wide = (F + 2) * H
    keep = jnp.where(me > 0, 1.0, 0.0)

    def columns(r, carry):
        left = jnp.concatenate(
            [
                jnp.concatenate(
                    [
                        rolled[r, t % 3, pl.ds((t // 3) * H, wide), pl.ds(128 * b, 128)]
                        for b in range(4)
                    ],
                    axis=0,
                )
                for t in range(8)
            ],
            axis=1,
        )
        for pair in range(2):
            both = jnp.dot(
                left, band[:, pl.ds(pair * 2 * C, 2 * C)], preferred_element_type=f32
            )
            for c in range(2):
                h0 = (both[:, c * C : (c + 1) * C] + b_in[...][None, :]).astype(bf16)
                values = h0.astype(f32)
                scale = lax.rsqrt(jnp.mean(values * values, axis=-1, keepdims=True) + 1e-06)
                half = values * (0.5 * scale) * gain[...][None, :]
                act = half + half * jnp.tanh(half)
                for b in range(4):
                    w = 8 * b + 4 * r + 2 * pair + c
                    d0, d1, d2, d3 = (
                        act[b * wide + f * H : b * wide + (f + 1) * H] for f in range(4)
                    )
                    d0, d1 = d0 * keep, d1 * keep
                    mixed[0, w + 1] = (d0 - d2).astype(bf16)
                    mixed[1, w + 1] = (0.5 * (d1 + d2)).astype(bf16)
                    mixed[2, w + 1] = (0.5 * (d2 - d1)).astype(bf16)
                    mixed[3, w + 1] = (d1 - d3).astype(bf16)
                    for a in range(F):
                        hid[w, a] = h0[b * wide + (a + 2) * H : b * wide + (a + 3) * H]
        return carry

    for r in range(2):
        columns(r, 0)

    after = lax.rem(me + 1, n)

    own, halo = (own_a, own_b), (halo_a, halo_b)

    def halo_copies(h, p):
        slots = [(h * 3 + f, (h, f)) for f in range(F)] if p == 0 else [(h * 3 + 2, (h,))]
        return [
            pltpu.make_async_remote_copy(
                src_ref=own[p].at[here], dst_ref=halo[p].at[here],
                send_sem=halo_send.at[slot], recv_sem=halo_recv.at[slot],
                device_id={"tm": after}, device_id_type=MESH,
            )
            for slot, here in slots
        ]

    rows = HALF * H

    def residual(h, carry):
        w0 = pl.multiple_of(h * HALF, HALF)
        for p, (c0, width) in enumerate(PARTS):
            def multiply(m, c0=c0, width=width):
                left = jnp.concatenate(
                    [mixed[m, pl.ds(w0 + dj, HALF)].reshape(rows, C) for dj in range(3)], axis=1
                )
                product[m, :, pl.ds(0, 3 * width)] = jnp.dot(
                    left,
                    jnp.concatenate(
                        [wmid[m, di, :, pl.ds(c0, width)] for di in range(3)], axis=1
                    ),
                    preferred_element_type=f32,
                )

            split = p == 0
            row = lax.broadcasted_iota(jnp.int32, (rows, width), 0) & (H - 1)
            for f in range(F):
                for m in ((1, 2, 0), (3,))[f] if split else ((1, 2, 0, 3), ())[f]:
                    multiply(m)
                p0, p1, p2, p3 = (product[m, :, pl.ds(0, 3 * width)] for m in range(4))
                three = p0 + p1 + p2 if f == 0 else p1 - p2 - p3
                above = pltpu.roll(three[:, :width], 1, 0)
                below = pltpu.roll(three[:, 2 * width :], rows - 1, 0)
                acc = hid[pl.ds(w0, HALF), f, :, pl.ds(c0, width)].astype(f32).reshape(rows, width)
                acc = acc + b_mid[pl.ds(c0, width)][None, :] + three[:, width : 2 * width]
                acc = acc + jnp.where(row == 0, 0.0, above) + jnp.where(row == H - 1, 0.0, below)
                for c in range(width // 128):
                    turn[f * 2 + c] = acc[:, c * 128 : (c + 1) * 128]
                for i in range(H):
                    line = [
                        turn[f * 2 + c, pl.ds(i, HALF, stride=H), :] for c in range(width // 128)
                    ]
                    own[p][h, f, i] = jnp.concatenate(
                        line, axis=1
                    ).astype(bf16)

                if split or f == F - 1:
                    @pl.when(me < n - 1)
                    def _():
                        for copy in halo_copies(h, p)[f if split else 0 :][:1]:
                            copy.start()

        return carry

    lax.fori_loop(0, 2, residual, 0)

    wtime_copy.wait()

    def both(pair, h, f):
        return jnp.concatenate(
            [ref[h, f].reshape(rows, width) for ref, (_, width) in zip(pair, PARTS)], axis=1
        )

    for h in range(2):
        mine0, mine1 = (both(own, h, f) for f in range(F))
        part[0, h] = b_time[...][None, :] + jnp.dot(
            mine0, wtime[pl.ds(2 * C, C)], preferred_element_type=f32
        )
        part[1, h] = b_time[...][None, :] + jnp.dot(
            jnp.concatenate([mine0, mine1], axis=1), wtime[pl.ds(C, 2 * C)],
            preferred_element_type=f32,
        )

    def sent_all(o, carry):
        lat_copy(other(o), me).wait_send()
        return carry

    lax.fori_loop(1, n, sent_all, 0)

    def gather(h, p):
        for copy in halo_copies(h, p):
            copy.wait_recv()
        if (h, p) != (1, 1):
            c0, width = PARTS[p]
            past0, past1 = (halo[p][h, f].reshape(rows, width) for f in range(F))
            part[0, h] += jnp.dot(
                jnp.concatenate([past0, past1], axis=1),
                jnp.concatenate([wtime[pl.ds(f * C + c0, width)] for f in range(F)], axis=0),
                preferred_element_type=f32,
            )
            part[1, h] += jnp.dot(past1, wtime[pl.ds(c0, width)], preferred_element_type=f32)

    @pl.when(me > 0)
    def _():
        gather(0, 0)
        gather(0, 1)

    for f in range(F):
        up = part[f, 0].astype(bf16)
        for s in range(2):
            ready[2 * f + s] = up[:, s * C : (s + 1) * C].reshape(H, HALF, C)

    @pl.when(me > 0)
    def _():
        gather(1, 0)
        gather(1, 1)

    @pl.when(me == 0)
    def _():
        halo_b[1] = jnp.zeros(halo_b.shape[1:], bf16)

    @pl.when(me < n - 1)
    def _():
        for h in range(2):
            for p in range(2):
                for copy in halo_copies(h, p):
                    copy.wait_send()


def finish(part, halo_b, wtime, ready, out_ref, staged, out_sem):
    rows = HALF * H

    def out_copy(h, e):
        return pltpu.make_async_copy(
            (ready, staged)[h].at[e], out_ref.at[e, :, pl.ds(h * HALF, HALF)], out_sem.at[h, e]
        )

    def put(h, f, up):
        up = up.astype(jnp.bfloat16)
        for s in range(2):
            staged[2 * f + s] = up[:, s * C : (s + 1) * C].reshape(H, HALF, C)
            out_copy(h, 2 * f + s).start()

    for e in range(2 * F):
        out_copy(0, e).start()
    c0, width = PARTS[1]
    past0, past1 = (halo_b[1, f].reshape(rows, width) for f in range(F))
    put(
        1, 1,
        part[1, 1]
        + jnp.dot(past1, wtime[pl.ds(c0, width)], preferred_element_type=jnp.float32),
    )
    put(
        1, 0,
        part[0, 1]
        + jnp.dot(
            jnp.concatenate([past0, past1], axis=1),
            jnp.concatenate([wtime[pl.ds(f * C + c0, width)] for f in range(F)], axis=0),
            preferred_element_type=jnp.float32,
        ),
    )
    for h in range(2):
        for e in range(2 * F):
            out_copy(h, e).wait()


def per_device(n, latent, w_in, b_in, gain, w_mid, b_mid, w_time, b_time):
    frames, block = latent.shape
    assert frames == F * n
    bf16, f32 = jnp.bfloat16, jnp.float32
    packed = block * 3 // 4 if block == 512 else block
    vmem = pl.BlockSpec(memory_space=pltpu.VMEM)
    hbm = pl.BlockSpec(memory_space=pltpu.HBM)
    dma = pltpu.SemaphoreType.DMA
    handed = pl.pallas_call(
        functools.partial(kernel, n),
        out_shape=(
            pltpu.VMEM((F, 2, HALF * H, 2 * C), f32),
            pltpu.VMEM((2, F, H, HALF, 128), bf16),
            pltpu.VMEM((3 * C, 2 * C), bf16),
            pltpu.VMEM((2 * F, H, HALF, C), bf16),
        ),
        in_specs=[hbm] * 8,
        out_specs=[vmem] * 4,
        scratch_shapes=[
            pltpu.VMEM((C,), f32), pltpu.VMEM((C,), f32), pltpu.VMEM((C,), f32),
            pltpu.VMEM((2 * C,), f32),
            pltpu.VMEM((frames, block), bf16),
            pltpu.VMEM((frames + 16, block), f32),
            pltpu.VMEM((n, 8, packed), bf16),
            pltpu.VMEM((n, 8, packed), bf16),
            pltpu.VMEM((block // 128, n * 8, 128), f32),
            pltpu.VMEM((2, 3, (F + 4) * H, ROW), bf16),
            pltpu.VMEM((9, 3 * ZC, C), bf16),
            pltpu.VMEM((8 * 128, GROUP * C), bf16),
            pltpu.VMEM((4, 3, 3 * C, C), bf16),
            pltpu.VMEM((4, W + 2, H, C), bf16),
            pltpu.VMEM((W, F, H, C), bf16),
            pltpu.VMEM((4, HALF * H, 3 * 256), f32),
            pltpu.VMEM((4, HALF * H, 128), f32),
            pltpu.VMEM((2, F, H, HALF, 256), bf16), pltpu.VMEM((2, F, H, HALF, 128), bf16),
            pltpu.VMEM((2, F, H, HALF, 256), bf16),
            dma((n,)), dma((n,)), dma((6,)), dma((6,)), dma(()), dma((9,)), dma(()), dma(()), dma((4,)),
        ],
        compiler_params=pltpu.CompilerParams(
            collective_id=0, has_side_effects=True, vmem_limit_bytes=44000000
        ),
        name="decoder_window",
    )(
        *(
            pltpu.with_memory_space_constraint(x, pltpu.HBM)
            for x in (
                latent, w_in.reshape(9, 3 * ZC, C), b_in, gain, w_mid.reshape(3, 3, 3 * C, C), b_mid,
                w_time.reshape(3 * C, 2 * C), b_time,
            )
        )
    )
    handed = [pltpu.with_memory_space_constraint(x, pltpu.VMEM) for x in handed]
    return pl.pallas_call(
        finish,
        out_shape=jax.ShapeDtypeStruct((2 * F, H, W, C), bf16),
        in_specs=[vmem] * 4,
        out_specs=hbm,
        scratch_shapes=[pltpu.VMEM((2 * F, H, HALF, C), bf16), dma((2, 2 * F))],
        compiler_params=pltpu.CompilerParams(vmem_limit_bytes=44000000),
        name="finish",
    )(*handed)


def solution(mesh):
    n = mesh.shape["tm"]
    return jax.shard_map(
        functools.partial(per_device, n),
        mesh=mesh,
        in_specs=(P("groups", "tm"), P(), P(), P(), P(), P(), P(), P()),
        out_specs=P(("groups", "tm"), None, None, None),
        check_vma=False,
    )
```

```python
import functools

import jax
import jax.numpy as jnp
from jax import lax
from jax.experimental import pallas as pl
from jax.experimental.pallas import tpu as pltpu
from jax.sharding import PartitionSpec as P

ZC = 16
C = 384
H = 16
W = 32
F = 2
ROW = W * ZC
WIDE = ROW + 128
GROUP = 4
HALF = W // 2
PARTS = ((0, 256), (256, 128))
MESH = pl.DeviceIdType.MESH


def kernel(
    n, latent_ref, w_in_ref, b_in_ref, gain_ref, w_mid_ref, b_mid_ref, w_time_ref, b_time_ref,
    part, halo_b, wtime, ready,
    b_in, gain, b_mid, b_time, mine, padded, sent, got, spread, rolled, win, band, wmid, mixed, hid, product, turn, own_a, own_b, halo_a,
    lat_send, lat_recv, halo_send, halo_recv, win_sem, wmid_sem, wtime_sem, mine_sem, vec_sem,
):
    bf16, f32 = jnp.bfloat16, jnp.float32
    me = lax.axis_index("tm")
    block = latent_ref.shape[1]
    frames = latent_ref.shape[0]
    per_row = ROW // block
    packed = sent.shape[2]

    mine_copy = pltpu.make_async_copy(latent_ref, mine, mine_sem)
    mine_copy.start()

    win_copy = pltpu.make_async_copy(w_in_ref, win, win_sem)
    vectors = ((b_in_ref, b_in), (gain_ref, gain), (b_mid_ref, b_mid), (b_time_ref, b_time))
    vec_copies = [
        pltpu.make_async_copy(src, dst, vec_sem.at[v]) for v, (src, dst) in enumerate(vectors)
    ]
    mid_copies = [
        [
            pltpu.make_async_copy(
                w_mid_ref.at[dt, di], wmid.at[(0, 1, 3)[dt], di], wmid_sem.at[di * 3 + dt]
            )
            for dt in range(3)
        ]
        for di in range(3)
    ]
    wtime_copy = pltpu.make_async_copy(w_time_ref, wtime, wtime_sem)

    def fetch():
        win_copy.start()
        for copy in vec_copies:
            copy.start()
        for copies in mid_copies:
            for copy in copies:
                copy.start()
        wtime_copy.start()

    barrier = pltpu.get_barrier_semaphore()

    def other(o):
        return lax.rem(me + o, n)

    quad = me - lax.rem(me, 4)
    first = [(c, k) for c in (3, 1, 2, 0)[:2] for k in range(1, n // 4)]
    last = [(c, k) for c in (3, 1, 2, 0)[2:] for k in range(1, n // 4)]
    targets = [lax.rem(quad + 4 * k + c, n) for c, k in first]
    targets += [quad + lax.rem(me + j, 4) for j in range(1, 4)]
    targets += [lax.rem(quad + 4 * k + c, n) for c, k in last]

    def greet(o, carry):
        pl.semaphore_signal(barrier, inc=1, device_id={"tm": other(o)}, device_id_type=MESH)
        return carry

    for o in range(1, n):
        greet(o, 0)
    fetch()

    padded[pl.ds(0, 8), :] = jnp.zeros((8, block), f32)
    padded[pl.ds(frames, 16), :] = jnp.zeros((16, block), f32)
    mine_copy.wait()
    padded[pl.ds(4, frames), :] = mine[...].astype(f32)
    for d in range(n):
        window = padded[pl.ds(F * d, 8), :]
        if packed < block:
            last = window[:, packed:]
            row = lax.broadcasted_iota(jnp.int32, (8, 128), 0)
            window = jnp.concatenate(
                [
                    jnp.where(
                        row < F + 4, window[:, c * 128 : (c + 1) * 128],
                        pltpu.roll(last, 6 - 2 * c, 0),
                    )
                    for c in range(3)
                ],
                axis=1,
            )
        sent[d] = window.astype(bf16)

    def combine(di):
        for copy in mid_copies[di]:
            copy.wait()

        def step(q, carry):
            here = (di, pl.ds(pl.multiple_of(q * 64, 64), 64))
            outer = wmid[0, *here].astype(f32) + wmid[3, *here].astype(f32)
            inner = wmid[1, *here].astype(f32)
            wmid[1, *here] = (outer + inner).astype(bf16)
            wmid[2, *here] = (outer - inner).astype(bf16)
            return carry

        lax.fori_loop(0, 3 * C // 64, step, 0)

    pl.semaphore_wait(barrier, n - 1)

    def lat_copy(d, j):
        return pltpu.make_async_remote_copy(
            src_ref=sent.at[d], dst_ref=got.at[j], send_sem=lat_send.at[d],
            recv_sem=lat_recv.at[j], device_id={"tm": d}, device_id_type=MESH,
        )

    for d in targets:
        lat_copy(d, me).start()

    def clear(t, carry):
        band[pl.ds(t * 128, 128), :] = jnp.zeros((128, GROUP * C), bf16)
        return carry

    lax.fori_loop(0, 8, clear, 0)
    for m in range(4):
        mixed[m, 0] = jnp.zeros((H, C), bf16)
        mixed[m, W + 1] = jnp.zeros((H, C), bf16)
    got[me] = sent[me]
    win_copy.wait()
    for c in range(GROUP):
        for t in range(8):
            band[pl.ds(t * 128 + ZC * c, 3 * ZC), pl.ds(c * C, C)] = win[t]
        for dj in range(3):
            third, odd = divmod(c + dj, 2)
            band[pl.ds(third * 128 + 96 + ZC * odd, ZC), pl.ds(c * C, C)] = win[8, pl.ds(ZC * dj, ZC)]
    for copy in vec_copies:
        copy.wait()

    for di in range(0, 3):
        combine(di)

    def receive(o, carry):
        lat_copy(other(o), other(o)).wait_recv()
        return carry

    for o in range(1, n):
        receive(o, 0)

    flat = got[...].astype(f32).reshape(n * 8, packed)
    for c in range(packed // 128):
        spread[c] = flat[:, c * 128 : (c + 1) * 128]
    picked = []
    for s in range(F + 4):
        parts = [
            spread[c, pl.ds(b * 8 + s, H, stride=8 * per_row), :]
            if c < packed // 128
            else spread[s // 2, pl.ds(b * 8 + 6 + s % 2, H, stride=8 * per_row), :]
            for b in range(per_row)
            for c in range(block // 128)
        ]
        parts.append(jnp.zeros((H, 128), f32))
        picked.append(jnp.concatenate(parts, axis=1))
    lat = jnp.concatenate(picked, axis=0)
    total = (F + 4) * H
    row_of = lax.broadcasted_iota(jnp.int32, (total, ROW), 0) & (H - 1)
    lane_of = lax.broadcasted_iota(jnp.int32, (total, ROW), 1) & 127
    for r in range(2):
        turned = pltpu.roll(lat, (ZC, WIDE - 3 * ZC)[r], 1)[:, :ROW]
        moved = (
            jnp.where(row_of == 0, 0.0, pltpu.roll(turned, 1, 0)),
            turned,
            jnp.where(row_of == H - 1, 0.0, pltpu.roll(turned, total - 1, 0)),
        )
        ninth = jnp.concatenate([moved[2][2 * H :], moved[2][: 2 * H]], axis=0)
        for di in range(3):
            third = pltpu.roll(ninth, 96 - 32 * di, 1)
            rolled[r, di] = jnp.where(lane_of < 96, moved[di], third).astype(bf16)

    wide = (F + 2) * H
    keep = jnp.where(me > 0, 1.0, 0.0)

    def columns(r, carry):
        left = jnp.concatenate(
            [
                jnp.concatenate(
                    [
                        rolled[r, t % 3, pl.ds((t // 3) * H, wide), pl.ds(128 * b, 128)]
                        for b in range(4)
                    ],
                    axis=0,
                )
                for t in range(8)
            ],
            axis=1,
        )
        for pair in range(2):
            both = jnp.dot(
                left, band[:, pl.ds(pair * 2 * C, 2 * C)], preferred_element_type=f32
            )
            for c in range(2):
                h0 = (both[:, c * C : (c + 1) * C] + b_in[...][None, :]).astype(bf16)
                values = h0.astype(f32)
                scale = lax.rsqrt(jnp.mean(values * values, axis=-1, keepdims=True) + 1e-06)
                half = values * (0.5 * scale) * gain[...][None, :]
                act = half + half * jnp.tanh(half)
                for b in range(4):
                    w = 8 * b + 4 * r + 2 * pair + c
                    d0, d1, d2, d3 = (
                        act[b * wide + f * H : b * wide + (f + 1) * H] for f in range(4)
                    )
                    d0, d1 = d0 * keep, d1 * keep
                    mixed[0, w + 1] = (d0 - d2).astype(bf16)
                    mixed[1, w + 1] = (0.5 * (d1 + d2)).astype(bf16)
                    mixed[2, w + 1] = (0.5 * (d2 - d1)).astype(bf16)
                    mixed[3, w + 1] = (d1 - d3).astype(bf16)
                    for a in range(F):
                        hid[w, a] = h0[b * wide + (a + 2) * H : b * wide + (a + 3) * H]
        return carry

    for r in range(2):
        columns(r, 0)

    after = lax.rem(me + 1, n)

    own, halo = (own_a, own_b), (halo_a, halo_b)

    def halo_copy(h, p):
        return pltpu.make_async_remote_copy(
            src_ref=own[p].at[h], dst_ref=halo[p].at[h],
            send_sem=halo_send.at[h * 2 + p], recv_sem=halo_recv.at[h * 2 + p],
            device_id={"tm": after}, device_id_type=MESH,
        )

    rows = HALF * H

    def residual(h, carry):
        w0 = pl.multiple_of(h * HALF, HALF)
        for p, (c0, width) in enumerate(PARTS):
            for m in range(4):
                left = jnp.concatenate(
                    [mixed[m, pl.ds(w0 + dj, HALF)].reshape(rows, C) for dj in range(3)], axis=1
                )
                product[m, :, pl.ds(0, 3 * width)] = jnp.dot(
                    left,
                    jnp.concatenate(
                        [wmid[m, di, :, pl.ds(c0, width)] for di in range(3)], axis=1
                    ),
                    preferred_element_type=f32,
                )
            p0, p1, p2, p3 = (product[m, :, pl.ds(0, 3 * width)] for m in range(4))
            row = lax.broadcasted_iota(jnp.int32, (rows, width), 0) & (H - 1)
            for f, three in enumerate((p0 + p1 + p2, p1 - p2 - p3)):
                above = pltpu.roll(three[:, :width], 1, 0)
                below = pltpu.roll(three[:, 2 * width :], rows - 1, 0)
                acc = hid[pl.ds(w0, HALF), f, :, pl.ds(c0, width)].astype(f32).reshape(rows, width)
                acc = acc + b_mid[pl.ds(c0, width)][None, :] + three[:, width : 2 * width]
                acc = acc + jnp.where(row == 0, 0.0, above) + jnp.where(row == H - 1, 0.0, below)
                for c in range(width // 128):
                    turn[f * 2 + c] = acc[:, c * 128 : (c + 1) * 128]
                for i in range(H):
                    line = [
                        turn[f * 2 + c, pl.ds(i, HALF, stride=H), :] for c in range(width // 128)
                    ]
                    own[p][h, f, i] = jnp.concatenate(
                        line, axis=1
                    ).astype(bf16)

            @pl.when(me < n - 1)
            def _():
                halo_copy(h, p).start()

        return carry

    lax.fori_loop(0, 2, residual, 0)

    wtime_copy.wait()

    def both(pair, h, f):
        return jnp.concatenate(
            [ref[h, f].reshape(rows, width) for ref, (_, width) in zip(pair, PARTS)], axis=1
        )

    for h in range(2):
        mine0, mine1 = (both(own, h, f) for f in range(F))
        part[0, h] = b_time[...][None, :] + jnp.dot(
            mine0, wtime[pl.ds(2 * C, C)], preferred_element_type=f32
        )
        part[1, h] = b_time[...][None, :] + jnp.dot(
            jnp.concatenate([mine0, mine1], axis=1), wtime[pl.ds(C, 2 * C)],
            preferred_element_type=f32,
        )

    def sent_all(o, carry):
        lat_copy(other(o), me).wait_send()
        return carry

    lax.fori_loop(1, n, sent_all, 0)

    def gather(h, p):
        halo_copy(h, p).wait_recv()
        if (h, p) != (1, 1):
            c0, width = PARTS[p]
            past0, past1 = (halo[p][h, f].reshape(rows, width) for f in range(F))
            part[0, h] += jnp.dot(
                jnp.concatenate([past0, past1], axis=1),
                jnp.concatenate([wtime[pl.ds(f * C + c0, width)] for f in range(F)], axis=0),
                preferred_element_type=f32,
            )
            part[1, h] += jnp.dot(past1, wtime[pl.ds(c0, width)], preferred_element_type=f32)

    @pl.when(me > 0)
    def _():
        gather(0, 0)
        gather(0, 1)

    for f in range(F):
        up = part[f, 0].astype(bf16)
        for s in range(2):
            ready[2 * f + s] = up[:, s * C : (s + 1) * C].reshape(H, HALF, C)

    @pl.when(me > 0)
    def _():
        gather(1, 0)
        gather(1, 1)

    @pl.when(me == 0)
    def _():
        halo_b[1] = jnp.zeros(halo_b.shape[1:], bf16)

    @pl.when(me < n - 1)
    def _():
        for h in range(2):
            for p in range(2):
                halo_copy(h, p).wait_send()


def finish(part, halo_b, wtime, ready, out_ref, staged, out_sem):
    rows = HALF * H

    def out_copy(h, e):
        return pltpu.make_async_copy(
            (ready, staged)[h].at[e], out_ref.at[e, :, pl.ds(h * HALF, HALF)], out_sem.at[h, e]
        )

    def put(h, f, up):
        up = up.astype(jnp.bfloat16)
        for s in range(2):
            staged[2 * f + s] = up[:, s * C : (s + 1) * C].reshape(H, HALF, C)
            out_copy(h, 2 * f + s).start()

    for e in range(2 * F):
        out_copy(0, e).start()
    c0, width = PARTS[1]
    past0, past1 = (halo_b[1, f].reshape(rows, width) for f in range(F))
    put(
        1, 1,
        part[1, 1]
        + jnp.dot(past1, wtime[pl.ds(c0, width)], preferred_element_type=jnp.float32),
    )
    put(
        1, 0,
        part[0, 1]
        + jnp.dot(
            jnp.concatenate([past0, past1], axis=1),
            jnp.concatenate([wtime[pl.ds(f * C + c0, width)] for f in range(F)], axis=0),
            preferred_element_type=jnp.float32,
        ),
    )
    for h in range(2):
        for e in range(2 * F):
            out_copy(h, e).wait()


def per_device(n, latent, w_in, b_in, gain, w_mid, b_mid, w_time, b_time):
    frames, block = latent.shape
    assert frames == F * n
    bf16, f32 = jnp.bfloat16, jnp.float32
    packed = block * 3 // 4 if block == 512 else block
    vmem = pl.BlockSpec(memory_space=pltpu.VMEM)
    hbm = pl.BlockSpec(memory_space=pltpu.HBM)
    dma = pltpu.SemaphoreType.DMA
    handed = pl.pallas_call(
        functools.partial(kernel, n),
        out_shape=(
            pltpu.VMEM((F, 2, HALF * H, 2 * C), f32),
            pltpu.VMEM((2, F, H, HALF, 128), bf16),
            pltpu.VMEM((3 * C, 2 * C), bf16),
            pltpu.VMEM((2 * F, H, HALF, C), bf16),
        ),
        in_specs=[hbm] * 8,
        out_specs=[vmem] * 4,
        scratch_shapes=[
            pltpu.VMEM((C,), f32), pltpu.VMEM((C,), f32), pltpu.VMEM((C,), f32),
            pltpu.VMEM((2 * C,), f32),
            pltpu.VMEM((frames, block), bf16),
            pltpu.VMEM((frames + 16, block), f32),
            pltpu.VMEM((n, 8, packed), bf16),
            pltpu.VMEM((n, 8, packed), bf16),
            pltpu.VMEM((block // 128, n * 8, 128), f32),
            pltpu.VMEM((2, 3, (F + 4) * H, ROW), bf16),
            pltpu.VMEM((9, 3 * ZC, C), bf16),
            pltpu.VMEM((8 * 128, GROUP * C), bf16),
            pltpu.VMEM((4, 3, 3 * C, C), bf16),
            pltpu.VMEM((4, W + 2, H, C), bf16),
            pltpu.VMEM((W, F, H, C), bf16),
            pltpu.VMEM((4, HALF * H, 3 * 256), f32),
            pltpu.VMEM((4, HALF * H, 128), f32),
            pltpu.VMEM((2, F, H, HALF, 256), bf16), pltpu.VMEM((2, F, H, HALF, 128), bf16),
            pltpu.VMEM((2, F, H, HALF, 256), bf16),
            dma((n,)), dma((n,)), dma((4,)), dma((4,)), dma(()), dma((9,)), dma(()), dma(()), dma((4,)),
        ],
        compiler_params=pltpu.CompilerParams(
            collective_id=0, has_side_effects=True, vmem_limit_bytes=44000000
        ),
        name="decoder_window",
    )(
        *(
            pltpu.with_memory_space_constraint(x, pltpu.HBM)
            for x in (
                latent, w_in.reshape(9, 3 * ZC, C), b_in, gain, w_mid.reshape(3, 3, 3 * C, C), b_mid,
                w_time.reshape(3 * C, 2 * C), b_time,
            )
        )
    )
    handed = [pltpu.with_memory_space_constraint(x, pltpu.VMEM) for x in handed]
    return pl.pallas_call(
        finish,
        out_shape=jax.ShapeDtypeStruct((2 * F, H, W, C), bf16),
        in_specs=[vmem] * 4,
        out_specs=hbm,
        scratch_shapes=[pltpu.VMEM((2 * F, H, HALF, C), bf16), dma((2, 2 * F))],
        compiler_params=pltpu.CompilerParams(vmem_limit_bytes=44000000),
        name="finish",
    )(*handed)


def solution(mesh):
    n = mesh.shape["tm"]
    return jax.shard_map(
        functools.partial(per_device, n),
        mesh=mesh,
        in_specs=(P("groups", "tm"), P(), P(), P(), P(), P(), P(), P()),
        out_specs=P(("groups", "tm"), None, None, None),
        check_vma=False,
    )
```
